32 devices in a mesh: dp: 2 (over x), seq: 4 (over z), tensor: 4 (over y, core).
Axes of the slice: x: 2, y: 2, z: 4, core: 2. Of those that a mesh axis runs over, the one named last changes fastest.
Arguments:
- tokens: float32 [4, 512, 768], P('dp', 'seq'), may hold values from -8 to 8
- positions: int32 [4, 512], P('dp', 'seq'), may hold values from 0 to 509, as said below
- qkv_weight: bfloat16 [768, 3, 768], P(('dp', 'seq'), None, 'tensor'), may hold values from -2 to 2
- attn_out_weight: bfloat16 [768, 768], P('tensor', ('dp', 'seq')), may hold values from -0.75 to 0.75
- mlp_in_weight: bfloat16 [768, 2, 1152], P(('dp', 'seq'), None, 'tensor'), may hold values from -0.21875 to 0.21875
- mlp_out_weight: bfloat16 [1152, 768], P('tensor', ('dp', 'seq')), may hold values from -0.1875 to 0.1875
- attn_gain: bfloat16 [768], P(('dp', 'seq')), may hold values from 0.25 to 1.75
- mlp_gain: bfloat16 [768], P(('dp', 'seq')), may hold values from 0.25 to 1.75
- cotangent: float32 [4, 512, 768], P('dp', 'seq'), may hold values from -6 to 6
Outputs:
- output: float32 [4, 512, 768], P('dp', 'seq')
- grad_tokens: float32 [4, 512, 768], P('dp', 'seq')
- grad_qkv: float32 [768, 3, 768], P(('dp', 'seq'), None, 'tensor')
- grad_attn_out: float32 [768, 768], P('tensor', ('dp', 'seq'))
- grad_mlp_in: float32 [768, 2, 1152], P(('dp', 'seq'), None, 'tensor')
- grad_mlp_out: float32 [1152, 768], P('tensor', ('dp', 'seq'))
- grad_attn_gain: float32 [768], P(('dp', 'seq'))
- grad_mlp_gain: float32 [768], P(('dp', 'seq'))
The draws below stay inside these ranges and needn't reach their ends.
Inputs may be any that keep to these rules, and one draw needn't show every extreme that they name: Each sequence packs three documents: the first ends within the first 64 positions, the last begins within the last 64 positions; a position counts the tokens before it in its own document.
All inputs are finite; a program needn't handle non-finite values.
Results may differ from the reference program's by a relative error of at most 0.014.
Values may be sent and summed in bfloat16 or wider, within the bound.
A program may use at most 128 MiB of HBM per device.

```python
import math
import jax
import jax.numpy as jnp
from jax import lax

D = 768
HEADS = 12
HD = 64
FF = 1152
LEN = 512
SEQS = 4


def draw_positions(key, part):
    first_result = jax.random.randint(jax.random.fold_in(key, 21), (SEQS, 1), 1, LEN // 8 + 1)
    last = jax.random.randint(jax.random.fold_in(key, 22), (SEQS, 1), LEN - LEN // 8, LEN)
    chosen_row = jax.random.randint(jax.random.fold_in(key, 23), (), 0, SEQS)
    row_index = jnp.arange(SEQS, dtype=jnp.int32)[:, None]
    first_result = jnp.where(row_index == chosen_row, 1, first_result)
    last = jnp.where(row_index == chosen_row, LEN - 1, last)
    index = jnp.broadcast_to(jnp.arange(LEN, dtype=jnp.int32)[None, :], (SEQS, LEN))
    begin = jnp.where(index >= last, last, jnp.where(index >= first_result, first_result, 0))
    return (index - begin).astype(jnp.int32)


def draw_tokens(key, part):
    values = jax.random.normal(jax.random.fold_in(key, 1), (SEQS, LEN, D), jnp.float32)
    return jnp.clip(values, -8.0, 8.0)


def draw_qkv_weight(key, part):
    values = jax.random.normal(jax.random.fold_in(key, 4), (D, 3, D), jnp.float32) * (1.0 / math.sqrt(D))
    return jnp.clip(values, -2.0, 2.0).astype(jnp.bfloat16)


def strengthened(entries, own_key, source, target, shards_of, factor):
    owner, partner = [(jnp.arange(entries.shape[position]) // (entries.shape[position] // shards_of)).reshape([-1 if axis == position else 1 for axis in range(entries.ndim)]) for position in (source, target)]
    chosen = jax.random.permutation(own_key, shards_of)[partner]
    strong = (owner == chosen) | (owner == (partner + shards_of // 2) % shards_of)
    return jnp.where(strong, factor * entries, entries)


def level_of(key, extent, pieces, low, top_value):
    loudness = 1.0
    for dim, parts in pieces:
        heights = jax.random.uniform(jax.random.fold_in(jax.random.fold_in(key, 6), dim), (parts,), jnp.float32, low / len(pieces), top_value / len(pieces))
        loudness = loudness * jnp.repeat(jnp.exp(heights), extent[dim] // parts).reshape((-1,) + (1,) * (len(extent) - 1 - dim))
    return loudness


def noise(own_key, shape, scale, bound, shards=(), held_as=jnp.bfloat16):
    values = jax.random.normal(own_key, shape, jnp.float32) * scale
    if len(shards) > 0:
        values = level_of(own_key, shape, shards, -0.22, 0.18) * values
    return jnp.clip(values, min=-bound, max=bound).astype(held_as)


def heavy_noise(key, dims, scale, limit, split, heavy, kind=jnp.bfloat16):
    values = scale * jax.random.normal(key, dims, jnp.float32)
    if split:
        values = values * level_of(key, dims, split, -0.22, 0.18)
    return jnp.clip(strengthened(values, jax.random.fold_in(key, 3), *heavy), -limit, limit).astype(kind)


def setup_inputs(seed: int = 0) -> dict:
    key_list = jax.random.split(jax.random.key(seed), 10)
    return {
        "tokens": draw_tokens(jax.random.fold_in(key_list[9], 71), 0),
        "positions": draw_positions(jax.random.fold_in(key_list[9], 71), 0),
        "qkv_weight": draw_qkv_weight(jax.random.fold_in(key_list[9], 71), 0),
        "attn_out_weight": noise(key_list[3], (D, D), HD ** -0.5, 0.75, ((0, 4), (1, 8))),
        "mlp_in_weight": noise(key_list[4], (D, 2, FF), D ** -0.5, 0.21875, ((0, 8), (2, 4))),
        "mlp_out_weight": noise(key_list[5], (FF, D), FF ** -0.5, 0.1875, ((0, 4), (1, 8))),
        "attn_gain": jnp.clip(1.0 + 0.15 * jax.random.normal(key_list[6], (D,), jnp.float32), 0.25, 1.75).astype(jnp.bfloat16),
        "mlp_gain": jnp.clip(1.0 + 0.15 * jax.random.normal(key_list[7], (D,), jnp.float32), 0.25, 1.75).astype(jnp.bfloat16),
        "cotangent": heavy_noise(key_list[8], (SEQS, LEN, D), 1.0, 6.0, ((0, 2), (1, 4)), (1, 2, 4, 2.0), jnp.float32),
    }


EPS = 1e-05
ROPE_BASE = 160000.0
INV_ROOT2 = 0.7071067811865476
INV_ROOT2PI = 0.3989422804014327

def apply_layer_norm(values):
    row_average = lax.optimization_barrier(jnp.mean(values, axis=-1, keepdims=True))
    centred = values - row_average
    inverse_deviation = lax.rsqrt(lax.optimization_barrier(jnp.mean(centred * centred, axis=-1, keepdims=True)) + EPS)
    return (centred * inverse_deviation, inverse_deviation)

def norm_backward_pass(centered_gradient, standardized_input, inverse_deviation):
    first_result = lax.optimization_barrier(jnp.mean(centered_gradient, axis=-1, keepdims=True))
    second_result = lax.optimization_barrier(jnp.mean(centered_gradient * standardized_input, axis=-1, keepdims=True))
    return inverse_deviation * (centered_gradient - first_result - standardized_input * second_result)

def rope_tables(places, width):
    half = width // 2
    ramp = jnp.arange(half, dtype=jnp.float32) * (2.0 / width)
    freq = jnp.exp(-math.log(ROPE_BASE) * ramp)
    angle = places.astype(jnp.float32)[:, None] * freq[None, :]
    cosine = jnp.cos(angle)
    sine = jnp.sin(angle)
    return (jnp.concatenate([cosine, cosine], axis=-1), jnp.concatenate([sine, sine], axis=-1))

def rotate(values, cosine, sine):
    half = values.shape[-1] // 2
    turned = jnp.concatenate([-values[..., half:], values[..., :half]], axis=-1)
    return values * cosine[:, None, :] + turned * sine[:, None, :]

def unrotate(grads, cosine, sine):
    half = grads.shape[-1] // 2
    moved = grads * sine[:, None, :]
    back = jnp.concatenate([moved[..., half:], -moved[..., :half]], axis=-1)
    return grads * cosine[:, None, :] + back

def gelu_parts(input_rows):
    cdf = 0.5 * (1.0 + jax.scipy.special.erf(input_rows * INV_ROOT2))
    return (input_rows * cdf, cdf + input_rows * jnp.exp(-0.5 * input_rows * input_rows) * INV_ROOT2PI)

def masked_scores(queries, keys, q_start, k_start):
    scale = 1.0 / math.sqrt(queries.shape[-1])
    scores = jnp.dot(queries, keys.T, preferred_element_type=jnp.float32) * scale
    return jnp.where(q_start[:, None] == k_start[None, :], scores, -jnp.inf)

def head_forward(queries, keys, values, q_start, k_start):
    scores = masked_scores(queries, keys, q_start, k_start)
    top = lax.optimization_barrier(jnp.max(scores, axis=-1, keepdims=True))
    lse = top[:, 0] + jnp.log(lax.optimization_barrier(jnp.sum(jnp.exp(scores - top), axis=-1)))
    probs = jnp.exp(scores - lse[:, None]).astype(jnp.bfloat16)
    context = jnp.dot(probs, values, preferred_element_type=jnp.float32).astype(jnp.bfloat16)
    return (context, lse)

def score_grads(queries, keys, values, dcontext, lse, delta, q_start, k_start):
    scale = 1.0 / math.sqrt(queries.shape[-1])
    scores = masked_scores(queries, keys, q_start, k_start)
    probs = jnp.exp(scores - lse[:, None])
    dprobs = jnp.dot(dcontext, values.T, preferred_element_type=jnp.float32)
    dscores = (probs * (dprobs - delta[:, None]) * scale).astype(jnp.bfloat16)
    return (probs.astype(jnp.bfloat16), dscores)

def one_sequence(input_rows, places, output_gradient, weights):
    qkv_weight, attn_out_weight, mlp_in_weight, mlp_out_weight, attn_gain, mlp_gain = weights
    block = min(512, LEN)
    nblock = LEN // block
    starts = jnp.arange(LEN, dtype=jnp.int32) - places.astype(jnp.int32)
    start_blocks = starts.reshape(nblock, block)
    cosine, sine = rope_tables(places, HD)
    attention_standardized, attention_inverse_deviation = apply_layer_norm(input_rows)
    attention_norm_gain = attn_gain.astype(jnp.float32)
    attention_normed = (attention_standardized * attention_norm_gain).astype(jnp.bfloat16)
    wide_qkv = qkv_weight.reshape(D, 3 * D)
    qkv = jnp.dot(attention_normed, wide_qkv, preferred_element_type=jnp.float32).reshape(LEN, 3, HEADS, HD)
    query = rotate(qkv[:, 0], cosine, sine).astype(jnp.bfloat16)
    key_rot = rotate(qkv[:, 1], cosine, sine).astype(jnp.bfloat16)
    value = qkv[:, 2].astype(jnp.bfloat16)
    q_heads = jnp.transpose(query, (1, 0, 2))
    k_heads = jnp.transpose(key_rot, (1, 0, 2))
    v_heads = jnp.transpose(value, (1, 0, 2))

    def forward_head(group):
        qx, kx, vx = group
        blocks = qx.reshape(nblock, block, HD)
        context, lse = lax.map(lambda item: head_forward(item[0], kx, vx, item[1], starts), (blocks, start_blocks))
        return (context.reshape(LEN, HD), lse.reshape(LEN))
    ctx_heads, lse_heads = lax.map(forward_head, (q_heads, k_heads, v_heads))
    context = jnp.transpose(ctx_heads, (1, 0, 2)).reshape(LEN, D)
    middle_state = input_rows + jnp.dot(context, attn_out_weight, preferred_element_type=jnp.float32)
    feedforward_standardized, feedforward_inverse_deviation = apply_layer_norm(middle_state)
    feedforward_norm_gain = mlp_gain.astype(jnp.float32)
    feedforward_normed = (feedforward_standardized * feedforward_norm_gain).astype(jnp.bfloat16)
    wide_in = mlp_in_weight.reshape(D, 2 * FF)
    upper = jnp.dot(feedforward_normed, wide_in, preferred_element_type=jnp.float32).reshape(LEN, 2, FF)
    active, slope = gelu_parts(upper[:, 0])
    gate = upper[:, 1]
    hidden = (active * gate).astype(jnp.bfloat16)
    output = middle_state + jnp.dot(hidden, mlp_out_weight, preferred_element_type=jnp.float32)
    dyb = output_gradient.astype(jnp.bfloat16)
    g_mlp_out = jnp.dot(hidden.T, dyb, preferred_element_type=jnp.float32)
    dhidden = jnp.dot(dyb, mlp_out_weight.T, preferred_element_type=jnp.float32)
    dup = jnp.stack([dhidden * gate * slope, dhidden * active], axis=1).astype(jnp.bfloat16).reshape(LEN, 2 * FF)
    g_mlp_in = jnp.dot(feedforward_normed.T, dup, preferred_element_type=jnp.float32).reshape(D, 2, FF)
    feedforward_normed_gradient = jnp.dot(dup, wide_in.T, preferred_element_type=jnp.float32)
    feedforward_gain_gradient = lax.optimization_barrier(jnp.sum(feedforward_normed_gradient * feedforward_standardized, axis=0))
    middle_gradient = output_gradient + norm_backward_pass(feedforward_normed_gradient * feedforward_norm_gain, feedforward_standardized, feedforward_inverse_deviation)
    dmidb = middle_gradient.astype(jnp.bfloat16)
    g_attn_out = jnp.dot(context.T, dmidb, preferred_element_type=jnp.float32)
    dcontext = jnp.dot(dmidb, attn_out_weight.T, preferred_element_type=jnp.float32).astype(jnp.bfloat16)
    dc_heads = jnp.transpose(dcontext.reshape(LEN, HEADS, HD), (1, 0, 2))
    delta_heads = lax.optimization_barrier(jnp.sum(dc_heads.astype(jnp.float32) * ctx_heads.astype(jnp.float32), axis=-1))

    def backward_head(group):
        qx, kx, vx, dcx, lsex, deltax = group

        def step(carry, rows):
            dkey, dvalue = carry
            qb, dcb, lb, db, sb = rows
            probs, dscores = score_grads(qb, kx, vx, dcb, lb, db, sb, starts)
            dquery = jnp.dot(dscores, kx, preferred_element_type=jnp.float32)
            dkey = dkey + jnp.dot(dscores.T, qb, preferred_element_type=jnp.float32)
            dvalue = dvalue + jnp.dot(probs.T, dcb, preferred_element_type=jnp.float32)
            return ((dkey, dvalue), dquery)
        start = (jnp.zeros((LEN, HD), jnp.float32), jnp.zeros((LEN, HD), jnp.float32))
        rows = (qx.reshape(nblock, block, HD), dcx.reshape(nblock, block, HD), lsex.reshape(nblock, block), deltax.reshape(nblock, block), start_blocks)
        (dkey, dvalue), dquery = lax.scan(step, start, rows)
        return (dquery.reshape(LEN, HD), dkey, dvalue)
    dq_heads, dk_heads, dv_heads = lax.map(backward_head, (q_heads, k_heads, v_heads, dc_heads, lse_heads, delta_heads))
    dquery = unrotate(jnp.transpose(dq_heads, (1, 0, 2)), cosine, sine)
    dkey = unrotate(jnp.transpose(dk_heads, (1, 0, 2)), cosine, sine)
    dvalue = jnp.transpose(dv_heads, (1, 0, 2))
    dqkv = jnp.stack([dquery, dkey, dvalue], axis=1).astype(jnp.bfloat16).reshape(LEN, 3 * D)
    g_qkv = jnp.dot(attention_normed.T, dqkv, preferred_element_type=jnp.float32).reshape(D, 3, D)
    attention_normed_gradient = jnp.dot(dqkv, wide_qkv.T, preferred_element_type=jnp.float32)
    attention_gain_gradient = lax.optimization_barrier(jnp.sum(attention_normed_gradient * attention_standardized, axis=0))
    input_gradient = middle_gradient + norm_backward_pass(attention_normed_gradient * attention_norm_gain, attention_standardized, attention_inverse_deviation)
    return (output, input_gradient, (g_qkv, g_attn_out, g_mlp_in, g_mlp_out, attention_gain_gradient, feedforward_gain_gradient))

def reference(tokens, positions, qkv_weight, attn_out_weight, mlp_in_weight, mlp_out_weight, attn_gain, mlp_gain, cotangent):
    weights = (qkv_weight, attn_out_weight, mlp_in_weight, mlp_out_weight, attn_gain, mlp_gain)
    start = (jnp.zeros((D, 3, D), jnp.float32), jnp.zeros((D, D), jnp.float32), jnp.zeros((D, 2, FF), jnp.float32), jnp.zeros((FF, D), jnp.float32), jnp.zeros((D,), jnp.float32), jnp.zeros((D,), jnp.float32))

    def step(carry, item):
        input_rows, places, output_gradient = item
        output, input_gradient, grads = one_sequence(input_rows, places, output_gradient, weights)
        carry = tuple((total + part for total, part in zip(carry, grads)))
        return (carry, (output, input_gradient))
    grads, (output, input_gradient) = lax.scan(step, start, (tokens, positions, cotangent))
    return (output, input_gradient, grads[0], grads[1], grads[2], grads[3], grads[4], grads[5])
```

```python
import math

import jax
import jax.numpy as jnp
from jax import lax
from jax.experimental import pallas as pl
from jax.experimental.pallas import tpu as pltpu
from jax.sharding import PartitionSpec as P

D = 768
HD = 64
EPS = 1e-05
ROPE_BASE = 160000.0
INV_ROOT2 = 0.7071067811865476
INV_ROOT2PI = 0.3989422804014327
MESH = pl.DeviceIdType.MESH
BF = jnp.bfloat16
F32 = jnp.float32
VM = pl.BlockSpec(memory_space=pltpu.VMEM)


def layer_norm(values):
    mean = jnp.mean(values, axis=-1, keepdims=True)
    centred = values - mean
    inverse = lax.rsqrt(jnp.mean(centred * centred, axis=-1, keepdims=True) + EPS)
    return centred * inverse, inverse


def norm_backward(e, xhat, r):
    first = jnp.mean(e, axis=-1, keepdims=True)
    second = jnp.mean(e * xhat, axis=-1, keepdims=True)
    return r * (e - first - xhat * second)


def rope_tables(places):
    half = HD // 2
    ramp = jnp.arange(half, dtype=F32) * (2.0 / HD)
    freq = jnp.exp(-math.log(ROPE_BASE) * ramp)
    angle = places.astype(F32)[:, None] * freq[None, :]
    cosine, sine = jnp.cos(angle), jnp.sin(angle)
    return jnp.concatenate([cosine, cosine], axis=-1), jnp.concatenate([sine, sine], axis=-1)


def rotate(values, cosine, sine):
    half = HD // 2
    turned = jnp.concatenate([-values[..., half:], values[..., :half]], axis=-1)
    return values * cosine[:, None, :] + turned * sine[:, None, :]


def unrotate(grads, cosine, sine):
    half = HD // 2
    moved = grads * sine[:, None, :]
    back = jnp.concatenate([moved[..., half:], -moved[..., :half]], axis=-1)
    return grads * cosine[:, None, :] + back


def gelu_parts(a):
    cdf = 0.5 * (1.0 + lax.erf(a * INV_ROOT2))
    return a * cdf, cdf + a * jnp.exp(-0.5 * a * a) * INV_ROOT2PI


def greet(axis, n):
    me = lax.axis_index(axis)
    barrier = pltpu.get_barrier_semaphore()
    for step in range(1, n):
        pl.semaphore_signal(
            barrier, inc=1, device_id={axis: lax.rem(me + step, n)}, device_id_type=MESH
        )
    pl.semaphore_wait(barrier, n - 1)
    return me


def push(src, dst, send, recv, axis, peer):
    copy = pltpu.make_async_remote_copy(
        src_ref=src, dst_ref=dst, send_sem=send, recv_sem=recv,
        device_id={axis: peer}, device_id_type=MESH,
    )
    copy.start()
    return copy


def gather_blocks(arrays, axis, n, cid):
    count = len(arrays)

    def kernel(*refs):
        ins, outs = refs[:count], refs[count : 2 * count]
        send, recv, local = refs[2 * count :]
        me = greet(axis, n)
        copies = []
        for i in range(count):
            for step in range(1, n):
                copies.append(
                    push(ins[i], outs[i].at[me], send.at[i, step], recv.at[i, step], axis,
                         lax.rem(me + step, n))
                )
        for i in range(count):
            own = pltpu.make_async_copy(ins[i], outs[i].at[me], local.at[i])
            own.start()
            own.wait()
        for copy in copies:
            copy.wait()

    return pl.pallas_call(
        kernel,
        out_shape=[jax.ShapeDtypeStruct((n,) + a.shape, a.dtype) for a in arrays],
        in_specs=[VM] * count,
        out_specs=[VM] * count,
        scratch_shapes=[
            pltpu.SemaphoreType.DMA((count, n)),
            pltpu.SemaphoreType.DMA((count, n)),
            pltpu.SemaphoreType.DMA((count,)),
        ],
        compiler_params=pltpu.CompilerParams(collective_id=cid, has_side_effects=True),
    )(*arrays)


def scatter_sum(blocks, axis, n, cid):
    shape = blocks.shape[1:]

    def kernel(in_ref, out_ref, land, send, recv):
        me = greet(axis, n)
        copies = [
            push(in_ref.at[lax.rem(me + step, n)], land.at[step - 1], send.at[step],
                 recv.at[step], axis, lax.rem(me + step, n))
            for step in range(1, n)
        ]
        total = in_ref[me].astype(F32)
        for step, copy in enumerate(copies):
            copy.wait()
            total = total + land[step].astype(F32)
        out_ref[...] = total

    return pl.pallas_call(
        kernel,
        out_shape=jax.ShapeDtypeStruct(shape, F32),
        in_specs=[VM],
        out_specs=VM,
        scratch_shapes=[
            pltpu.VMEM((n - 1,) + shape, blocks.dtype),
            pltpu.SemaphoreType.DMA((n,)),
            pltpu.SemaphoreType.DMA((n,)),
        ],
        compiler_params=pltpu.CompilerParams(collective_id=cid, has_side_effects=True),
    )(blocks)


def sum_rows_then_gather(partials, extras, middle, gathered, owned, axis, n, cid):
    np_, ne, ng, no = len(partials), len(extras), len(gathered), len(owned)
    rows = partials[0].shape[1:]

    def kernel(*refs):
        refs = list(refs)
        take = lambda k: [refs.pop(0) for _ in range(k)]
        parts, more, gouts, oouts, lands = take(np_), take(ne), take(ng), take(no), take(np_)
        send, recv, gsend, grecv = refs
        me = greet(axis, n)
        copies = []
        for i in range(np_):
            copies.append([
                push(parts[i].at[lax.rem(me + step, n)], lands[i].at[step - 1], send.at[i, step],
                     recv.at[i, step], axis, lax.rem(me + step, n))
                for step in range(1, n)
            ])
        sums = []
        for i in range(np_):
            total = parts[i][me].astype(F32)
            for step, copy in enumerate(copies[i]):
                copy.wait()
                total = total + lands[i][step].astype(F32)
            sums.append(total)
        shared, kept = middle(sums, [m[...] for m in more])
        copies = []
        for i in range(ng):
            gouts[i][me] = shared[i].astype(gathered[i][1])
            for step in range(1, n):
                copies.append(
                    push(gouts[i].at[me], gouts[i].at[me], gsend.at[i, step], grecv.at[i, step],
                         axis, lax.rem(me + step, n))
                )
        for i in range(no):
            oouts[i][...] = kept[i].astype(owned[i][1])
        for copy in copies:
            copy.wait()

    return pl.pallas_call(
        kernel,
        out_shape=[jax.ShapeDtypeStruct((n,) + s, t) for s, t in gathered]
        + [jax.ShapeDtypeStruct(s, t) for s, t in owned],
        in_specs=[VM] * (np_ + ne),
        out_specs=[VM] * (ng + no),
        scratch_shapes=[pltpu.VMEM((n - 1,) + rows, p.dtype) for p in partials]
        + [
            pltpu.SemaphoreType.DMA((np_, n)),
            pltpu.SemaphoreType.DMA((np_, n)),
            pltpu.SemaphoreType.DMA((ng, n)),
            pltpu.SemaphoreType.DMA((ng, n)),
        ],
        compiler_params=pltpu.CompilerParams(collective_id=cid, has_side_effects=True),
    )(*partials, *extras)


def dot(a, b):
    return jnp.dot(a, b, preferred_element_type=F32)


def dot_t(a, b):
    return lax.dot_general(a, b, (((1,), (1,)), ((), ())), preferred_element_type=F32)


def t_dot(a, b):
    return lax.dot_general(a, b, (((0,), (0,)), ((), ())), preferred_element_type=F32)


def make_per_device(mesh):
    n_seq, n_ten = mesh.shape["seq"], mesh.shape["tensor"]

    def per_device(tokens, positions, qkv_weight, attn_out_weight, mlp_in_weight, mlp_out_weight,
                   attn_gain, mlp_gain, cotangent):
        S, R = tokens.shape[:2]
        T, L = S * R, R * n_seq
        w, u = qkv_weight.shape[2], mlp_out_weight.shape[0]
        h = w // HD
        wr = qkv_weight.shape[0]
        own = T // n_ten
        group = ("dp", "seq")
        pack_a = jnp.concatenate(
            [qkv_weight.reshape(wr, 3 * w), attn_gain[:, None], mlp_gain[:, None]], axis=1)
        pack_b = jnp.concatenate(
            [attn_out_weight.T, mlp_in_weight.reshape(wr, 2 * u), mlp_out_weight.T], axis=1)
        full_a = lax.all_gather(pack_a, group, axis=0, tiled=True)
        full_b = lax.all_gather(pack_b, group, axis=0, tiled=True)
        w_qkv = full_a[:, : 3 * w]
        gain1 = full_a[:, 3 * w].astype(F32)[None, :]
        gain2 = full_a[:, 3 * w + 1].astype(F32)[None, :]
        w_out_t = full_b[:, :w]
        w_in = full_b[:, w : w + 2 * u]
        w_down_t = full_b[:, w + 2 * u :]

        x = tokens.reshape(T, D)
        cot = cotangent.reshape(T, D)
        dyb = cot.astype(BF)
        t_me = lax.axis_index("tensor")
        mine = lambda a: lax.dynamic_slice_in_dim(a, t_me * own, own, 0)
        x_own, cot_own = mine(x), mine(cot)

        index = lax.axis_index("seq") * R + jnp.arange(R, dtype=jnp.int32)
        starts = index[None, :] - positions
        cosine, sine = rope_tables(positions.reshape(T))

        xhat1, _ = layer_norm(x)
        normed1 = (xhat1 * gain1).astype(BF)
        qkv = dot(normed1, w_qkv).reshape(T, 3, h, HD)
        q = rotate(qkv[:, 0], cosine, sine).astype(BF)
        k = rotate(qkv[:, 1], cosine, sine).astype(BF)
        v = qkv[:, 2].astype(BF)
        kv = jnp.concatenate([k.reshape(T, w), v.reshape(T, w)], axis=1)
        starts8 = jnp.pad(starts, ((0, 8 - S), (0, 0)))
        kv_all, starts_all = gather_blocks([kv, starts8], "seq", n_seq, 0)
        k_start = jnp.transpose(starts_all[:, :S], (1, 0, 2)).reshape(S, L)
        kv_heads = jnp.transpose(
            kv_all.reshape(n_seq, S, R, 2, h, HD), (3, 1, 4, 0, 2, 5)).reshape(2, S, h, L, HD)
        keys, values = kv_heads[0], kv_heads[1]
        qh = jnp.transpose(q.reshape(S, R, h, HD), (0, 2, 1, 3))
        scale = 1.0 / math.sqrt(HD)
        mask = (starts[:, :, None] == k_start[:, None, :])[:, None]
        scores = jnp.einsum("shqd,shkd->shqk", qh, keys, preferred_element_type=F32) * scale
        scores = jnp.where(mask, scores, -jnp.inf)
        top = jnp.max(scores, axis=-1, keepdims=True)
        lse = top + jnp.log(jnp.sum(jnp.exp(scores - top), axis=-1, keepdims=True))
        probs32 = jnp.exp(scores - lse)
        probs = probs32.astype(BF)
        ctx_h = jnp.einsum("shqk,shkd->shqd", probs, values, preferred_element_type=F32).astype(BF)
        context = jnp.transpose(ctx_h, (0, 2, 1, 3)).reshape(T, w)

        mid_part = dot_t(context, w_out_t).astype(BF).reshape(n_ten, own, D)

        def after_attention(sums, more):
            mid = more[0] + sums[0]
            xhat2, _ = layer_norm(mid)
            return [xhat2 * more[1]], [mid]

        normed2, mid_own = sum_rows_then_gather(
            [mid_part], [x_own, gain2], after_attention,
            [((own, D), BF)], [((own, D), F32)], "tensor", n_ten, 1)
        normed2 = normed2.reshape(T, D)
        up = dot(normed2, w_in)
        active, slope = gelu_parts(up[:, :u])
        gate = up[:, u:]
        hidden = (active * gate).astype(BF)
        out_part = dot_t(hidden, w_down_t).astype(BF).reshape(n_ten, own, D)
        dhidden = dot(dyb, w_down_t)
        dup = jnp.concatenate([dhidden * gate * slope, dhidden * active], axis=1).astype(BF)
        dn2_part = dot_t(dup, w_in).astype(BF).reshape(n_ten, own, D)

        def after_mlp(sums, more):
            mid, dy, gain = more
            xhat2, rstd2 = layer_norm(mid)
            dn2, down = sums
            gain_grad = jnp.sum(dn2 * xhat2, axis=0, keepdims=True)
            dmid = dy + norm_backward(dn2 * gain, xhat2, rstd2)
            return [dmid, mid + down], [dmid, gain_grad]

        dmidb, out_rows, dmid_own, g_gain2 = sum_rows_then_gather(
            [dn2_part, out_part], [mid_own, cot_own, gain2], after_mlp,
            [((own, D), BF), ((own, D), BF)], [((own, D), F32), ((1, D), F32)],
            "tensor", n_ten, 2)
        output = out_rows.astype(F32).reshape(S, R, D)
        dmidb = dmidb.reshape(T, D)
        dcontext = dot(dmidb, w_out_t).astype(BF)
        g_b = jnp.concatenate([
            t_dot(dmidb, context).astype(BF),
            t_dot(normed2, dup).astype(BF),
            t_dot(dyb, hidden).astype(BF),
        ], axis=1)
        sum_b = lax.psum_scatter(g_b, group, scatter_dimension=0, tiled=True)

        dch = jnp.transpose(dcontext.reshape(S, R, h, HD), (0, 2, 1, 3))
        delta = jnp.sum(dch.astype(F32) * ctx_h.astype(F32), axis=-1, keepdims=True)
        dprobs = jnp.einsum("shqd,shkd->shqk", dch, values, preferred_element_type=F32)
        dscores = (probs32 * (dprobs - delta) * scale).astype(BF)
        dqh = jnp.einsum("shqk,shkd->shqd", dscores, keys, preferred_element_type=F32)
        dkh = jnp.einsum("shqk,shqd->shkd", dscores, qh, preferred_element_type=F32)
        dvh = jnp.einsum("shqk,shqd->shkd", probs, dch, preferred_element_type=F32)
        dkv = jnp.stack([dkh, dvh]).astype(BF).reshape(2, S, h, n_seq, R, HD)
        dkv = jnp.transpose(dkv, (3, 1, 4, 0, 2, 5)).reshape(n_seq, T, 2 * w)
        dkv_own = scatter_sum(dkv, "seq", n_seq, 3)
        dq = unrotate(jnp.transpose(dqh, (0, 2, 1, 3)).reshape(T, h, HD), cosine, sine)
        dk = unrotate(dkv_own[:, :w].reshape(T, h, HD), cosine, sine)
        dqkv = jnp.concatenate(
            [dq.reshape(T, w), dk.reshape(T, w), dkv_own[:, w:]], axis=1).astype(BF)
        dn1_part = dot_t(dqkv, w_qkv).astype(BF).reshape(n_ten, own, D)

        def at_the_end(sums, more):
            rows, dmid, gain, gain_grad2 = more
            xhat, rstd = layer_norm(rows)
            dn1 = sums[0]
            gain_grad1 = jnp.sum(dn1 * xhat, axis=0, keepdims=True)
            grad = dmid + norm_backward(dn1 * gain, xhat, rstd)
            pad = jnp.zeros((6, D), F32)
            return [jnp.concatenate([gain_grad1, gain_grad2, pad], axis=0), grad], []

        gains, grad_rows = sum_rows_then_gather(
            [dn1_part], [x_own, dmid_own, gain1, g_gain2], at_the_end,
            [((8, D), F32), ((own, D), BF)], [], "tensor", n_ten, 4)
        grad_tokens = grad_rows.astype(F32).reshape(S, R, D)
        gains = jnp.sum(gains[:, :2], axis=0)
        g_a = jnp.concatenate([t_dot(normed1, dqkv).astype(BF), gains.T.astype(BF)], axis=1)
        sum_a = lax.psum_scatter(g_a, group, scatter_dimension=0, tiled=True)
        sum_a, sum_b = sum_a.astype(F32), sum_b.astype(F32)
        return (
            output,
            grad_tokens,
            sum_a[:, : 3 * w].reshape(wr, 3, w),
            sum_b[:, :w].T,
            sum_b[:, w : w + 2 * u].reshape(wr, 2, u),
            sum_b[:, w + 2 * u :].T,
            sum_a[:, 3 * w],
            sum_a[:, 3 * w + 1],
        )

    return per_device


def solution(mesh):
    rows = P("dp", "seq", None)
    group = ("dp", "seq")
    weights = (P(group, None, "tensor"), P("tensor", group), P(group, None, "tensor"),
               P("tensor", group), P(group), P(group))
    return jax.shard_map(
        make_per_device(mesh), mesh=mesh,
        in_specs=(rows, P("dp", "seq")) + weights + (rows,),
        out_specs=(rows, rows) + weights,
        check_vma=False,
    )
```

```python
import math

import jax
import jax.numpy as jnp
from jax import lax
from jax.experimental import pallas as pl
from jax.experimental.pallas import tpu as pltpu
from jax.sharding import PartitionSpec as P

D = 768
HD = 64
EPS = 1e-05
ROPE_BASE = 160000.0
INV_ROOT2 = 0.7071067811865476
INV_ROOT2PI = 0.3989422804014327
MESH = pl.DeviceIdType.MESH
BF = jnp.bfloat16
F32 = jnp.float32
VM = pl.BlockSpec(memory_space=pltpu.VMEM)


def layer_norm(values):
    mean = jnp.mean(values, axis=-1, keepdims=True)
    centred = values - mean
    inverse = lax.rsqrt(jnp.mean(centred * centred, axis=-1, keepdims=True) + EPS)
    return centred * inverse, inverse


def norm_backward(e, xhat, r):
    first = jnp.mean(e, axis=-1, keepdims=True)
    second = jnp.mean(e * xhat, axis=-1, keepdims=True)
    return r * (e - first - xhat * second)


def rope_tables(places):
    half = HD // 2
    ramp = jnp.arange(half, dtype=F32) * (2.0 / HD)
    freq = jnp.exp(-math.log(ROPE_BASE) * ramp)
    angle = places.astype(F32)[:, None] * freq[None, :]
    cosine, sine = jnp.cos(angle), jnp.sin(angle)
    return jnp.concatenate([cosine, cosine], axis=-1), jnp.concatenate([sine, sine], axis=-1)


def rotate(values, cosine, sine):
    half = HD // 2
    turned = jnp.concatenate([-values[..., half:], values[..., :half]], axis=-1)
    return values * cosine[:, None, :] + turned * sine[:, None, :]


def unrotate(grads, cosine, sine):
    half = HD // 2
    moved = grads * sine[:, None, :]
    back = jnp.concatenate([moved[..., half:], -moved[..., :half]], axis=-1)
    return grads * cosine[:, None, :] + back


def gelu_parts(a):
    cdf = 0.5 * (1.0 + lax.erf(a * INV_ROOT2))
    return a * cdf, cdf + a * jnp.exp(-0.5 * a * a) * INV_ROOT2PI


def greet(*names_and_sizes):
    barrier = pltpu.get_barrier_semaphore()
    count = 0
    for axis, n in names_and_sizes:
        me = lax.axis_index(axis)
        for step in range(1, n):
            pl.semaphore_signal(
                barrier, inc=1, device_id={axis: lax.rem(me + step, n)}, device_id_type=MESH
            )
            count += 1
    pl.semaphore_wait(barrier, count)


def push(src, dst, send, recv, axis, peer):
    copy = pltpu.make_async_remote_copy(
        src_ref=src, dst_ref=dst, send_sem=send, recv_sem=recv,
        device_id={axis: peer}, device_id_type=MESH,
    )
    copy.start()
    return copy


class WeightGather:
    def __init__(self, array, n_dp, n_seq):
        self.array, self.n_dp, self.n_seq = array, n_dp, n_seq
        self.outs = [jax.ShapeDtypeStruct((n_dp * n_seq,) + array.shape, array.dtype)]
        sem = pltpu.SemaphoreType.DMA
        self.scratch = [sem((n_seq,)), sem((n_seq,)), sem((n_dp, n_seq)), sem((n_dp, n_seq)), sem((1,))]

    def across(self, src, block, step):
        dp = lax.axis_index("dp")
        return [
            push(src, self.out.at[block], self.xs.at[k, step], self.xr.at[k, step], "dp",
                 lax.rem(dp + k, self.n_dp))
            for k in range(1, self.n_dp)
        ]

    def begin(self, src, outs, scratch):
        (self.out,) = outs
        zs, zr, self.xs, self.xr, local = scratch
        seq = lax.axis_index("seq")
        self.base = lax.axis_index("dp") * self.n_seq
        block = self.base + seq
        self.along = [
            push(src, self.out.at[block], zs.at[step], zr.at[step], "seq",
                 lax.rem(seq + step, self.n_seq))
            for step in range(1, self.n_seq)
        ]
        self.crossing = self.across(src, block, 0)
        self.own = pltpu.make_async_copy(src, self.out.at[block], local.at[0])
        self.own.start()

    def end(self):
        seq = lax.axis_index("seq")
        for step, copy in enumerate(self.along, 1):
            copy.wait_recv()
            block = self.base + lax.rem(seq + self.n_seq - step, self.n_seq)
            self.crossing += self.across(self.out.at[block], block, step)
        for copy in self.along:
            copy.wait_send()
        for copy in self.crossing:
            copy.wait()
        self.own.wait()


class GradScatter:
    def __init__(self, array, n_dp, n_seq):
        self.array, self.n_dp, self.n_seq = array, n_dp, n_seq
        shape, kind = array.shape[1:], array.dtype
        self.outs = [jax.ShapeDtypeStruct(shape, F32)]
        sem = pltpu.SemaphoreType.DMA
        self.scratch = [
            pltpu.VMEM((n_dp - 1, n_seq) + shape, kind),
            pltpu.VMEM((n_seq,) + shape, kind),
            pltpu.VMEM((n_seq,) + shape, kind),
            sem((n_dp, n_seq)), sem((n_dp, n_seq)), sem((n_seq,)), sem((n_seq,)),
        ]

    def begin(self, src, outs, scratch):
        self.src, (self.out,) = src, outs
        self.landx, self.stage, self.landz, xs, xr, self.zs, self.zr = scratch
        dp, seq = lax.axis_index("dp"), lax.axis_index("seq")
        self.crossing = {}
        for step in list(range(1, self.n_seq)) + [0]:
            to = lax.rem(seq + step, self.n_seq)
            self.crossing[step] = [
                push(src.at[lax.rem(dp + k, self.n_dp) * self.n_seq + to],
                     self.landx.at[k - 1, step], xs.at[k, step], xr.at[k, step], "dp",
                     lax.rem(dp + k, self.n_dp))
                for k in range(1, self.n_dp)
            ]

    def end(self):
        dp, seq = lax.axis_index("dp"), lax.axis_index("seq")
        along = []
        for step in list(range(1, self.n_seq)) + [0]:
            to = lax.rem(seq + step, self.n_seq)
            total = self.src[dp * self.n_seq + to].astype(F32)
            for k, copy in enumerate(self.crossing[step]):
                copy.wait()
                total = total + self.landx[k, step].astype(F32)
            if step:
                self.stage[step] = total.astype(self.stage.dtype)
                along.append(
                    push(self.stage.at[step], self.landz.at[step], self.zs.at[step],
                         self.zr.at[step], "seq", to))
        for step, copy in enumerate(along, 1):
            copy.wait()
            total = total + self.landz[step].astype(F32)
        self.out[...] = total


class GainSum:
    def __init__(self, array, n_dp, n_seq, n_ten):
        self.array, self.sizes = array, (n_ten, n_dp, n_seq)
        shape = array.shape[1:]
        self.outs = [jax.ShapeDtypeStruct(shape, F32)]
        sem = pltpu.SemaphoreType.DMA
        self.scratch = [
            pltpu.VMEM((n_ten,) + array.shape, F32),
            pltpu.VMEM(array.shape, F32),
            pltpu.VMEM((n_dp, n_seq) + shape, F32),
            pltpu.VMEM((n_seq,) + shape, F32),
            pltpu.VMEM((n_seq,) + shape, F32),
        ] + [sem((n,)) for n in (n_ten, n_ten, n_seq, n_seq)] + [sem((n_dp, n_seq))] * 2

    def begin(self, src, outs, scratch):
        self.src, (self.out,) = src, outs
        (self.land, self.total, self.landx, self.stage, self.landz,
         ys, yr, self.zs, self.zr, self.xs, self.xr) = scratch
        n_ten = self.sizes[0]
        me = lax.axis_index("tensor")
        self.first = [
            push(src, self.land.at[step], ys.at[step], yr.at[step], "tensor",
                 lax.rem(me + step, n_ten))
            for step in range(1, n_ten)
        ]

    def between(self):
        _, n_dp, n_seq = self.sizes
        dp, seq = lax.axis_index("dp"), lax.axis_index("seq")
        total = self.src[...]
        for step, copy in enumerate(self.first, 1):
            copy.wait()
            total = total + self.land[step]
        self.total[...] = total
        self.crossing = {
            step: [
                push(self.total.at[lax.rem(dp + k, n_dp) * n_seq + lax.rem(seq + step, n_seq)],
                     self.landx.at[k, step], self.xs.at[k, step], self.xr.at[k, step], "dp",
                     lax.rem(dp + k, n_dp))
                for k in range(1, n_dp)
            ]
            for step in range(n_seq)
        }

    def end(self):
        _, n_dp, n_seq = self.sizes
        dp, seq = lax.axis_index("dp"), lax.axis_index("seq")
        along = []
        for step in list(range(1, n_seq)) + [0]:
            to = lax.rem(seq + step, n_seq)
            total = self.total[dp * n_seq + to]
            for k, copy in enumerate(self.crossing[step], 1):
                copy.wait()
                total = total + self.landx[k, step]
            if step:
                self.stage[step] = total
                along.append(
                    push(self.stage.at[step], self.landz.at[step], self.zs.at[step],
                         self.zr.at[step], "seq", to))
        for step, copy in enumerate(along, 1):
            copy.wait()
            total = total + self.landz[step]
        self.out[...] = total


def gather_weights(array, n_dp, n_seq, cid):
    job = WeightGather(array, n_dp, n_seq)

    def kernel(src, out, *scratch):
        greet(("dp", n_dp), ("seq", n_seq))
        job.begin(src, [out], scratch)
        job.end()

    return pl.pallas_call(
        kernel, out_shape=job.outs[0], in_specs=[VM], out_specs=VM, scratch_shapes=job.scratch,
        compiler_params=pltpu.CompilerParams(collective_id=cid, has_side_effects=True),
    )(array)


def gather_blocks(arrays, axis, n, cid):
    count = len(arrays)

    def kernel(*refs):
        ins, outs = refs[:count], refs[count : 2 * count]
        send, recv, local = refs[2 * count :]
        greet((axis, n))
        me = lax.axis_index(axis)
        copies = []
        for i in range(count):
            for step in range(1, n):
                copies.append(
                    push(ins[i], outs[i].at[me], send.at[i, step], recv.at[i, step], axis,
                         lax.rem(me + step, n))
                )
        for i in range(count):
            own = pltpu.make_async_copy(ins[i], outs[i].at[me], local.at[i])
            own.start()
            own.wait()
        for copy in copies:
            copy.wait()

    return pl.pallas_call(
        kernel,
        out_shape=[jax.ShapeDtypeStruct((n,) + a.shape, a.dtype) for a in arrays],
        in_specs=[VM] * count,
        out_specs=[VM] * count,
        scratch_shapes=[
            pltpu.SemaphoreType.DMA((count, n)),
            pltpu.SemaphoreType.DMA((count, n)),
            pltpu.SemaphoreType.DMA((count,)),
        ],
        compiler_params=pltpu.CompilerParams(collective_id=cid, has_side_effects=True),
    )(*arrays)


def scatter_sum(blocks, axis, n, cid):
    shape = blocks.shape[1:]

    def kernel(in_ref, out_ref, land, send, recv):
        greet((axis, n))
        me = lax.axis_index(axis)
        copies = [
            push(in_ref.at[lax.rem(me + step, n)], land.at[step - 1], send.at[step],
                 recv.at[step], axis, lax.rem(me + step, n))
            for step in range(1, n)
        ]
        total = in_ref[me].astype(F32)
        for step, copy in enumerate(copies):
            copy.wait()
            total = total + land[step].astype(F32)
        out_ref[...] = total

    return pl.pallas_call(
        kernel,
        out_shape=jax.ShapeDtypeStruct(shape, F32),
        in_specs=[VM],
        out_specs=VM,
        scratch_shapes=[
            pltpu.VMEM((n - 1,) + shape, blocks.dtype),
            pltpu.SemaphoreType.DMA((n,)),
            pltpu.SemaphoreType.DMA((n,)),
        ],
        compiler_params=pltpu.CompilerParams(collective_id=cid, has_side_effects=True),
    )(blocks)


def sum_rows_then_gather(partials, extras, middle, gathered, owned, sizes, jobs, cid):
    n_dp, n_seq, n = sizes
    np_, ne, ng, no, nj = len(partials), len(extras), len(gathered), len(owned), len(jobs)
    rows = partials[0].shape[1:]

    def kernel(*refs):
        refs = list(refs)
        take = lambda k: [refs.pop(0) for _ in range(k)]
        parts, more, srcs = take(np_), take(ne), take(nj)
        gouts, oouts, jouts = take(ng), take(no), take(nj)
        lands, (send, recv, gsend, grecv) = take(np_), take(4)
        greet(("dp", n_dp), ("seq", n_seq), ("tensor", n))
        me = lax.axis_index("tensor")
        copies = []
        for i in range(np_):
            copies.append([
                push(parts[i].at[lax.rem(me + step, n)], lands[i].at[step - 1], send.at[i, step],
                     recv.at[i, step], "tensor", lax.rem(me + step, n))
                for step in range(1, n)
            ])
        for job, src, out in zip(jobs, srcs, jouts):
            job.begin(src, [out], take(len(job.scratch)))
        sums = []
        for i in range(np_):
            total = parts[i][me].astype(F32)
            for step, copy in enumerate(copies[i]):
                copy.wait()
                total = total + lands[i][step].astype(F32)
            sums.append(total)
        shared, kept = middle(sums, [m[...] for m in more])
        copies = []
        for i in range(ng):
            gouts[i][me] = shared[i].astype(gathered[i][1])
            for step in range(1, n):
                copies.append(
                    push(gouts[i].at[me], gouts[i].at[me], gsend.at[i, step], grecv.at[i, step],
                         "tensor", lax.rem(me + step, n))
                )
        for i in range(no):
            oouts[i][...] = kept[i].astype(owned[i][1])
        for job in jobs:
            if isinstance(job, GainSum):
                job.between()
        for job in jobs:
            job.end()
        for copy in copies:
            copy.wait()

    sem = pltpu.SemaphoreType.DMA
    return pl.pallas_call(
        kernel,
        out_shape=[jax.ShapeDtypeStruct((n,) + s, t) for s, t in gathered]
        + [jax.ShapeDtypeStruct(s, t) for s, t in owned]
        + [job.outs[0] for job in jobs],
        in_specs=[VM] * (np_ + ne + nj),
        out_specs=[VM] * (ng + no + nj),
        scratch_shapes=[pltpu.VMEM((n - 1,) + rows, p.dtype) for p in partials]
        + [sem((np_, n)), sem((np_, n)), sem((ng, n)), sem((ng, n))]
        + [scratch for job in jobs for scratch in job.scratch],
        compiler_params=pltpu.CompilerParams(collective_id=cid, has_side_effects=True),
    )(*partials, *extras, *[job.array for job in jobs])


def dot(a, b):
    return jnp.dot(a, b, preferred_element_type=F32)


def dot_t(a, b):
    return lax.dot_general(a, b, (((1,), (1,)), ((), ())), preferred_element_type=F32)


def t_dot(a, b):
    return lax.dot_general(a, b, (((0,), (0,)), ((), ())), preferred_element_type=F32)


def make_per_device(mesh):
    n_dp, n_seq, n_ten = mesh.shape["dp"], mesh.shape["seq"], mesh.shape["tensor"]
    sizes = (n_dp, n_seq, n_ten)
    n_all = n_dp * n_seq

    def per_device(tokens, positions, qkv_weight, attn_out_weight, mlp_in_weight, mlp_out_weight,
                   attn_gain, mlp_gain, cotangent):
        S, R = tokens.shape[:2]
        T, L = S * R, R * n_seq
        w, u = qkv_weight.shape[2], mlp_out_weight.shape[0]
        h = w // HD
        wr = qkv_weight.shape[0]
        own = T // n_ten
        pack_a = jnp.concatenate(
            [qkv_weight.reshape(wr, 3 * w), attn_out_weight.T, attn_gain[:, None], mlp_gain[:, None]],
            axis=1)
        pack_b = jnp.concatenate([mlp_in_weight.reshape(wr, 2 * u), mlp_out_weight.T], axis=1)
        full_a = gather_weights(pack_a, n_dp, n_seq, 5).reshape(D, 4 * w + 2)
        w_qkv = full_a[:, : 3 * w]
        w_out_t = full_a[:, 3 * w : 4 * w]
        gain1 = full_a[:, 4 * w].astype(F32)[None, :]
        gain2 = full_a[:, 4 * w + 1].astype(F32)[None, :]

        x = tokens.reshape(T, D)
        cot = cotangent.reshape(T, D)
        dyb = cot.astype(BF)
        t_me = lax.axis_index("tensor")
        mine = lambda a: lax.dynamic_slice_in_dim(a, t_me * own, own, 0)
        x_own, cot_own = mine(x), mine(cot)

        index = lax.axis_index("seq") * R + jnp.arange(R, dtype=jnp.int32)
        starts = index[None, :] - positions
        cosine, sine = rope_tables(positions.reshape(T))

        xhat1, _ = layer_norm(x)
        normed1 = (xhat1 * gain1).astype(BF)
        qkv = dot(normed1, w_qkv).reshape(T, 3, h, HD)
        q = rotate(qkv[:, 0], cosine, sine).astype(BF)
        k = rotate(qkv[:, 1], cosine, sine).astype(BF)
        v = qkv[:, 2].astype(BF)
        kv = jnp.concatenate([k.reshape(T, w), v.reshape(T, w)], axis=1)
        starts8 = jnp.pad(starts, ((0, 8 - S), (0, 0)))
        kv_all, starts_all = gather_blocks([kv, starts8], "seq", n_seq, 0)
        k_start = jnp.transpose(starts_all[:, :S], (1, 0, 2)).reshape(S, L)
        kv_heads = jnp.transpose(
            kv_all.reshape(n_seq, S, R, 2, h, HD), (3, 1, 4, 0, 2, 5)).reshape(2, S, h, L, HD)
        keys, values = kv_heads[0], kv_heads[1]
        qh = jnp.transpose(q.reshape(S, R, h, HD), (0, 2, 1, 3))
        scale = 1.0 / math.sqrt(HD)
        mask = (starts[:, :, None] == k_start[:, None, :])[:, None]
        scores = jnp.einsum("shqd,shkd->shqk", qh, keys, preferred_element_type=F32) * scale
        scores = jnp.where(mask, scores, -jnp.inf)
        top = jnp.max(scores, axis=-1, keepdims=True)
        lse = top + jnp.log(jnp.sum(jnp.exp(scores - top), axis=-1, keepdims=True))
        probs32 = jnp.exp(scores - lse)
        probs = probs32.astype(BF)
        ctx_h = jnp.einsum("shqk,shkd->shqd", probs, values, preferred_element_type=F32).astype(BF)
        context = jnp.transpose(ctx_h, (0, 2, 1, 3)).reshape(T, w)

        mid_part = dot_t(context, w_out_t).astype(BF).reshape(n_ten, own, D)

        def after_attention(sums, more):
            mid = more[0] + sums[0]
            xhat2, _ = layer_norm(mid)
            return [xhat2 * more[1]], [mid]

        normed2, mid_own, full_b = sum_rows_then_gather(
            [mid_part], [x_own, gain2], after_attention,
            [((own, D), BF)], [((own, D), F32)], sizes,
            [WeightGather(pack_b, n_dp, n_seq)], 1)
        full_b = full_b.reshape(D, 3 * u)
        w_in, w_down_t = full_b[:, : 2 * u], full_b[:, 2 * u :]
        normed2 = normed2.reshape(T, D)
        up = dot(normed2, w_in)
        active, slope = gelu_parts(up[:, :u])
        gate = up[:, u:]
        hidden = (active * gate).astype(BF)
        out_part = dot_t(hidden, w_down_t).astype(BF).reshape(n_ten, own, D)
        dhidden = dot(dyb, w_down_t)
        dup = jnp.concatenate([dhidden * gate * slope, dhidden * active], axis=1).astype(BF)
        dn2_part = dot_t(dup, w_in).astype(BF).reshape(n_ten, own, D)

        def after_mlp(sums, more):
            mid, dy, gain = more
            xhat2, rstd2 = layer_norm(mid)
            dn2, down = sums
            gain_grad = jnp.sum(dn2 * xhat2, axis=0, keepdims=True)
            dmid = dy + norm_backward(dn2 * gain, xhat2, rstd2)
            return [dmid, mid + down], [dmid, gain_grad]

        g_b = jnp.concatenate([t_dot(normed2, dup).astype(BF), t_dot(dyb, hidden).astype(BF)], axis=1)
        dmidb, out_rows, dmid_own, g_gain2, sum_b = sum_rows_then_gather(
            [dn2_part, out_part], [mid_own, cot_own, gain2], after_mlp,
            [((own, D), BF), ((own, D), BF)], [((own, D), F32), ((1, D), F32)],
            sizes, [GradScatter(g_b.reshape(n_all, wr, 3 * u), n_dp, n_seq)], 2)
        output = out_rows.astype(F32).reshape(S, R, D)
        dmidb = dmidb.reshape(T, D)
        dcontext = dot(dmidb, w_out_t).astype(BF)
        dch = jnp.transpose(dcontext.reshape(S, R, h, HD), (0, 2, 1, 3))
        delta = jnp.sum(dch.astype(F32) * ctx_h.astype(F32), axis=-1, keepdims=True)
        dprobs = jnp.einsum("shqd,shkd->shqk", dch, values, preferred_element_type=F32)
        dscores = (probs32 * (dprobs - delta) * scale).astype(BF)
        dqh = jnp.einsum("shqk,shkd->shqd", dscores, keys, preferred_element_type=F32)
        dkh = jnp.einsum("shqk,shqd->shkd", dscores, qh, preferred_element_type=F32)
        dvh = jnp.einsum("shqk,shqd->shkd", probs, dch, preferred_element_type=F32)
        dkv = jnp.stack([dkh, dvh]).astype(BF).reshape(2, S, h, n_seq, R, HD)
        dkv = jnp.transpose(dkv, (3, 1, 4, 0, 2, 5)).reshape(n_seq, T, 2 * w)
        dkv_own = scatter_sum(dkv, "seq", n_seq, 3)
        dq = unrotate(jnp.transpose(dqh, (0, 2, 1, 3)).reshape(T, h, HD), cosine, sine)
        dk = unrotate(dkv_own[:, :w].reshape(T, h, HD), cosine, sine)
        dqkv = jnp.concatenate(
            [dq.reshape(T, w), dk.reshape(T, w), dkv_own[:, w:]], axis=1).astype(BF)
        dn1_part = dot_t(dqkv, w_qkv)
        g_gain1 = jnp.sum(dn1_part * xhat1, axis=0)
        dn1_part = dn1_part.astype(BF).reshape(n_ten, own, D)
        gain_grads = jnp.stack([g_gain1, g_gain2[0]]).reshape(2, n_all, wr)
        gain_grads = jnp.pad(jnp.transpose(gain_grads, (1, 0, 2)), ((0, 0), (0, 6), (0, 128 - wr)))
        g_a = jnp.concatenate([t_dot(normed1, dqkv).astype(BF), t_dot(dmidb, context).astype(BF)], axis=1)

        def at_the_end(sums, more):
            rows, dmid, gain = more
            xhat, rstd = layer_norm(rows)
            return [dmid + norm_backward(sums[0] * gain, xhat, rstd)], []

        grad_rows, sum_a, gains = sum_rows_then_gather(
            [dn1_part], [x_own, dmid_own, gain1], at_the_end,
            [((own, D), BF)], [], sizes,
            [GradScatter(g_a.reshape(n_all, wr, 4 * w), n_dp, n_seq),
             GainSum(gain_grads, n_dp, n_seq, n_ten)], 4)
        grad_tokens = grad_rows.astype(F32).reshape(S, R, D)
        return (
            output,
            grad_tokens,
            sum_a[:, : 3 * w].reshape(wr, 3, w),
            sum_a[:, 3 * w :].T,
            sum_b[:, : 2 * u].reshape(wr, 2, u),
            sum_b[:, 2 * u :].T,
            gains[0, :wr],
            gains[1, :wr],
        )

    return per_device


def solution(mesh):
    rows = P("dp", "seq", None)
    group = ("dp", "seq")
    weights = (P(group, None, "tensor"), P("tensor", group), P(group, None, "tensor"),
               P("tensor", group), P(group), P(group))
    return jax.shard_map(
        make_per_device(mesh), mesh=mesh,
        in_specs=(rows, P("dp", "seq")) + weights + (rows,),
        out_specs=(rows, rows) + weights,
        check_vma=False,
    )
```

```python
import math

import jax
import jax.numpy as jnp
from jax import lax
from jax.experimental import pallas as pl
from jax.experimental.pallas import tpu as pltpu
from jax.sharding import PartitionSpec as P

D = 768
HD = 64
EPS = 1e-05
ROPE_BASE = 160000.0
INV_ROOT2 = 0.7071067811865476
INV_ROOT2PI = 0.3989422804014327
MESH = pl.DeviceIdType.MESH
BF = jnp.bfloat16
F32 = jnp.float32
VM = pl.BlockSpec(memory_space=pltpu.VMEM)


def layer_norm(values):
    mean = jnp.mean(values, axis=-1, keepdims=True)
    centred = values - mean
    inverse = lax.rsqrt(jnp.mean(centred * centred, axis=-1, keepdims=True) + EPS)
    return centred * inverse, inverse


def norm_backward(e, xhat, r):
    first = jnp.mean(e, axis=-1, keepdims=True)
    second = jnp.mean(e * xhat, axis=-1, keepdims=True)
    return r * (e - first - xhat * second)


def rope_tables(places):
    half = HD // 2
    ramp = jnp.arange(half, dtype=F32) * (2.0 / HD)
    freq = jnp.exp(-math.log(ROPE_BASE) * ramp)
    angle = places.astype(F32)[:, None] * freq[None, :]
    cosine, sine = jnp.cos(angle), jnp.sin(angle)
    return jnp.concatenate([cosine, cosine], axis=-1), jnp.concatenate([sine, sine], axis=-1)


def rotate(values, cosine, sine):
    half = HD // 2
    turned = jnp.concatenate([-values[..., half:], values[..., :half]], axis=-1)
    return values * cosine[:, None, :] + turned * sine[:, None, :]


def unrotate(grads, cosine, sine):
    half = HD // 2
    moved = grads * sine[:, None, :]
    back = jnp.concatenate([moved[..., half:], -moved[..., :half]], axis=-1)
    return grads * cosine[:, None, :] + back


def gelu_parts(a):
    cdf = 0.5 * (1.0 + lax.erf(a * INV_ROOT2))
    return a * cdf, cdf + a * jnp.exp(-0.5 * a * a) * INV_ROOT2PI


def greet(*names_and_sizes):
    barrier = pltpu.get_barrier_semaphore()
    count = 0
    for axis, n in names_and_sizes:
        me = lax.axis_index(axis)
        for step in range(1, n):
            pl.semaphore_signal(
                barrier, inc=1, device_id={axis: lax.rem(me + step, n)}, device_id_type=MESH
            )
            count += 1
    pl.semaphore_wait(barrier, count)


def push(src, dst, send, recv, axis, peer):
    copy = pltpu.make_async_remote_copy(
        src_ref=src, dst_ref=dst, send_sem=send, recv_sem=recv,
        device_id={axis: peer}, device_id_type=MESH,
    )
    copy.start()
    return copy


class WeightGather:
    def __init__(self, array, n_dp, n_seq):
        self.array, self.n_dp, self.n_seq = array, n_dp, n_seq
        self.outs = [jax.ShapeDtypeStruct((n_dp * n_seq,) + array.shape, array.dtype)]
        sem = pltpu.SemaphoreType.DMA
        self.scratch = [sem((n_seq,)), sem((n_seq,)), sem((n_dp, n_seq)), sem((n_dp, n_seq)), sem((1,))]

    def across(self, src, block, step):
        dp = lax.axis_index("dp")
        return [
            push(src, self.out.at[block], self.xs.at[k, step], self.xr.at[k, step], "dp",
                 lax.rem(dp + k, self.n_dp))
            for k in range(1, self.n_dp)
        ]

    def begin(self, src, outs, scratch):
        (self.out,) = outs
        zs, zr, self.xs, self.xr, local = scratch
        seq = lax.axis_index("seq")
        self.base = lax.axis_index("dp") * self.n_seq
        block = self.base + seq
        self.along = [
            push(src, self.out.at[block], zs.at[step], zr.at[step], "seq",
                 lax.rem(seq + step, self.n_seq))
            for step in range(1, self.n_seq)
        ]
        self.crossing = self.across(src, block, 0)
        self.own = pltpu.make_async_copy(src, self.out.at[block], local.at[0])
        self.own.start()

    def end(self):
        seq = lax.axis_index("seq")
        for step, copy in enumerate(self.along, 1):
            copy.wait_recv()
            block = self.base + lax.rem(seq + self.n_seq - step, self.n_seq)
            self.crossing += self.across(self.out.at[block], block, step)
        for copy in self.along:
            copy.wait_send()
        for copy in self.crossing:
            copy.wait()
        self.own.wait()


class GradScatter:
    def __init__(self, array, n_dp, n_seq):
        self.array, self.n_dp, self.n_seq = array, n_dp, n_seq
        shape, kind = array.shape[1:], array.dtype
        self.outs = [jax.ShapeDtypeStruct(shape, F32)]
        sem = pltpu.SemaphoreType.DMA
        self.scratch = [
            pltpu.VMEM((n_dp - 1, n_seq) + shape, kind),
            pltpu.VMEM((n_seq,) + shape, kind),
            pltpu.VMEM((n_seq,) + shape, kind),
            sem((n_dp, n_seq)), sem((n_dp, n_seq)), sem((n_seq,)), sem((n_seq,)),
        ]

    def begin(self, src, outs, scratch):
        self.src, (self.out,) = src, outs
        self.landx, self.stage, self.landz, xs, xr, self.zs, self.zr = scratch
        dp, seq = lax.axis_index("dp"), lax.axis_index("seq")
        self.crossing = {}
        for step in list(range(1, self.n_seq)) + [0]:
            to = lax.rem(seq + step, self.n_seq)
            self.crossing[step] = [
                push(src.at[lax.rem(dp + k, self.n_dp) * self.n_seq + to],
                     self.landx.at[k - 1, step], xs.at[k, step], xr.at[k, step], "dp",
                     lax.rem(dp + k, self.n_dp))
                for k in range(1, self.n_dp)
            ]

    def end(self):
        dp, seq = lax.axis_index("dp"), lax.axis_index("seq")
        along = []
        for step in list(range(1, self.n_seq)) + [0]:
            to = lax.rem(seq + step, self.n_seq)
            total = self.src[dp * self.n_seq + to].astype(F32)
            for k, copy in enumerate(self.crossing[step]):
                copy.wait()
                total = total + self.landx[k, step].astype(F32)
            if step:
                self.stage[step] = total.astype(self.stage.dtype)
                along.append(
                    push(self.stage.at[step], self.landz.at[step], self.zs.at[step],
                         self.zr.at[step], "seq", to))
        for step, copy in enumerate(along, 1):
            copy.wait()
            total = total + self.landz[step].astype(F32)
        self.out[...] = total


class GainSum:
    def __init__(self, array, n_dp, n_seq, n_ten):
        self.array, self.sizes = array, (n_ten, n_dp, n_seq)
        shape = array.shape[1:]
        self.outs = [jax.ShapeDtypeStruct(shape, F32)]
        sem = pltpu.SemaphoreType.DMA
        self.scratch = [
            pltpu.VMEM((n_ten,) + array.shape, F32),
            pltpu.VMEM(array.shape, F32),
            pltpu.VMEM((n_dp, n_seq) + shape, F32),
            pltpu.VMEM((n_seq,) + shape, F32),
            pltpu.VMEM((n_seq,) + shape, F32),
        ] + [sem((n,)) for n in (n_ten, n_ten, n_seq, n_seq)] + [sem((n_dp, n_seq))] * 2

    def begin(self, src, outs, scratch):
        self.src, (self.out,) = src, outs
        (self.land, self.total, self.landx, self.stage, self.landz,
         ys, yr, self.zs, self.zr, self.xs, self.xr) = scratch
        n_ten = self.sizes[0]
        me = lax.axis_index("tensor")
        self.first = [
            push(src, self.land.at[step], ys.at[step], yr.at[step], "tensor",
                 lax.rem(me + step, n_ten))
            for step in range(1, n_ten)
        ]

    def between(self):
        _, n_dp, n_seq = self.sizes
        dp, seq = lax.axis_index("dp"), lax.axis_index("seq")
        total = self.src[...]
        for step, copy in enumerate(self.first, 1):
            copy.wait()
            total = total + self.land[step]
        self.total[...] = total
        self.crossing = {
            step: [
                push(self.total.at[lax.rem(dp + k, n_dp) * n_seq + lax.rem(seq + step, n_seq)],
                     self.landx.at[k, step], self.xs.at[k, step], self.xr.at[k, step], "dp",
                     lax.rem(dp + k, n_dp))
                for k in range(1, n_dp)
            ]
            for step in range(n_seq)
        }

    def end(self):
        _, n_dp, n_seq = self.sizes
        dp, seq = lax.axis_index("dp"), lax.axis_index("seq")
        along = []
        for step in list(range(1, n_seq)) + [0]:
            to = lax.rem(seq + step, n_seq)
            total = self.total[dp * n_seq + to]
            for k, copy in enumerate(self.crossing[step], 1):
                copy.wait()
                total = total + self.landx[k, step]
            if step:
                self.stage[step] = total
                along.append(
                    push(self.stage.at[step], self.landz.at[step], self.zs.at[step],
                         self.zr.at[step], "seq", to))
        for step, copy in enumerate(along, 1):
            copy.wait()
            total = total + self.landz[step]
        self.out[...] = total


def gather_weights(array, n_dp, n_seq, cid):
    job = WeightGather(array, n_dp, n_seq)

    def kernel(src, out, *scratch):
        greet(("dp", n_dp), ("seq", n_seq))
        job.begin(src, [out], scratch)
        job.end()

    return pl.pallas_call(
        kernel, out_shape=job.outs[0], in_specs=[VM], out_specs=VM, scratch_shapes=job.scratch,
        compiler_params=pltpu.CompilerParams(collective_id=cid, has_side_effects=True),
    )(array)


def scatter_sum(blocks, axis, n, cid):
    shape = blocks.shape[1:]

    def kernel(in_ref, out_ref, land, send, recv):
        greet((axis, n))
        me = lax.axis_index(axis)
        copies = [
            push(in_ref.at[lax.rem(me + step, n)], land.at[step - 1], send.at[step],
                 recv.at[step], axis, lax.rem(me + step, n))
            for step in range(1, n)
        ]
        total = in_ref[me].astype(F32)
        for step, copy in enumerate(copies):
            copy.wait()
            total = total + land[step].astype(F32)
        out_ref[...] = total

    return pl.pallas_call(
        kernel,
        out_shape=jax.ShapeDtypeStruct(shape, F32),
        in_specs=[VM],
        out_specs=VM,
        scratch_shapes=[
            pltpu.VMEM((n - 1,) + shape, blocks.dtype),
            pltpu.SemaphoreType.DMA((n,)),
            pltpu.SemaphoreType.DMA((n,)),
        ],
        compiler_params=pltpu.CompilerParams(collective_id=cid, has_side_effects=True),
    )(blocks)


def sum_rows_then_gather(partials, extras, middle, gathered, owned, sizes, jobs, cid):
    n_dp, n_seq, n = sizes
    np_, ne, ng, no, nj = len(partials), len(extras), len(gathered), len(owned), len(jobs)
    rows = partials[0].shape[1:]

    def kernel(*refs):
        refs = list(refs)
        take = lambda k: [refs.pop(0) for _ in range(k)]
        parts, more, srcs = take(np_), take(ne), take(nj)
        gouts, oouts, jouts = take(ng), take(no), take(nj)
        lands, (send, recv, gsend, grecv) = take(np_), take(4)
        greet(("dp", n_dp), ("seq", n_seq), ("tensor", n))
        me = lax.axis_index("tensor")
        copies = []
        for i in range(np_):
            copies.append([
                push(parts[i].at[lax.rem(me + step, n)], lands[i].at[step - 1], send.at[i, step],
                     recv.at[i, step], "tensor", lax.rem(me + step, n))
                for step in range(1, n)
            ])
        for job, src, out in zip(jobs, srcs, jouts):
            job.begin(src, [out], take(len(job.scratch)))
        sums = []
        for i in range(np_):
            total = parts[i][me].astype(F32)
            for step, copy in enumerate(copies[i]):
                copy.wait()
                total = total + lands[i][step].astype(F32)
            sums.append(total)
        shared, kept = middle(sums, [m[...] for m in more])
        copies = []
        for i in range(ng):
            gouts[i][me] = shared[i].astype(gathered[i][1])
            for step in range(1, n):
                copies.append(
                    push(gouts[i].at[me], gouts[i].at[me], gsend.at[i, step], grecv.at[i, step],
                         "tensor", lax.rem(me + step, n))
                )
        for i in range(no):
            oouts[i][...] = kept[i].astype(owned[i][1])
        for job in jobs:
            if isinstance(job, GainSum):
                job.between()
        for job in jobs:
            job.end()
        for copy in copies:
            copy.wait()

    sem = pltpu.SemaphoreType.DMA
    return pl.pallas_call(
        kernel,
        out_shape=[jax.ShapeDtypeStruct((n,) + s, t) for s, t in gathered]
        + [jax.ShapeDtypeStruct(s, t) for s, t in owned]
        + [job.outs[0] for job in jobs],
        in_specs=[VM] * (np_ + ne + nj),
        out_specs=[VM] * (ng + no + nj),
        scratch_shapes=[pltpu.VMEM((n - 1,) + rows, p.dtype) for p in partials]
        + [sem((np_, n)), sem((np_, n)), sem((ng, n)), sem((ng, n))]
        + [scratch for job in jobs for scratch in job.scratch],
        compiler_params=pltpu.CompilerParams(collective_id=cid, has_side_effects=True),
    )(*partials, *extras, *[job.array for job in jobs])


def dot(a, b):
    return jnp.dot(a, b, preferred_element_type=F32)


def dot_t(a, b):
    return lax.dot_general(a, b, (((1,), (1,)), ((), ())), preferred_element_type=F32)


def t_dot(a, b):
    return lax.dot_general(a, b, (((0,), (0,)), ((), ())), preferred_element_type=F32)


def attention_stage(kv, starts8, q, q_start, w_out_t, x_own, gain, pack_b, sizes, S, cid):
    n_dp, n_seq, n = sizes
    T, w = q.shape
    R, h, own = T // S, w // HD, x_own.shape[0]
    L = R * n_seq
    scale = 1.0 / math.sqrt(HD)
    job = WeightGather(pack_b, n_dp, n_seq)

    def kernel(kv_ref, st_ref, q_ref, qs_ref, wo_ref, x_ref, gain_ref, pb_ref,
               normed_out, mid_out, ctx_out, lse_out, kv_all, st_all, pb_out,
               part, land, ksend, krecv, local, send, recv, gsend, grecv, *rest):
        greet(("dp", n_dp), ("seq", n_seq), ("tensor", n))
        me, seq = lax.axis_index("tensor"), lax.axis_index("seq")
        arriving = []
        for i, (src, dst) in enumerate(((st_ref, st_all), (kv_ref, kv_all))):
            for step in range(1, n_seq):
                arriving.append(
                    push(src, dst.at[seq], ksend.at[i, step], krecv.at[i, step], "seq",
                         lax.rem(seq + step, n_seq)))
            mine = pltpu.make_async_copy(src, dst.at[seq], local.at[i])
            mine.start()
            mine.wait()
        job.begin(pb_ref, [pb_out], rest)
        for copy in arriving:
            copy.wait()
        for s in range(S):
            rows = slice(s * R, (s + 1) * R)
            k_start = jnp.concatenate([st_all[j, s : s + 1, :] for j in range(n_seq)], axis=1)
            same = qs_ref[rows, :] == k_start
            heads = []
            for i in range(h):
                cols = slice(i * HD, (i + 1) * HD)
                keys = kv_all[:, rows, cols].reshape(L, HD)
                values = kv_all[:, rows, w + i * HD : w + (i + 1) * HD].reshape(L, HD)
                scores = jnp.where(same, dot_t(q_ref[rows, cols], keys) * scale, -jnp.inf)
                top = jnp.max(scores, axis=-1, keepdims=True)
                lse = top + jnp.log(jnp.sum(jnp.exp(scores - top), axis=-1, keepdims=True))
                lse_out[s * h + i] = lse
                probs = jnp.exp(scores - lse).astype(BF)
                heads.append(dot(probs, values).astype(BF))
            ctx_out[rows, :] = jnp.concatenate(heads, axis=1)
        projected = dot_t(ctx_out[...], wo_ref[...]).astype(BF)
        for i in range(n):
            part[i] = projected[i * own : (i + 1) * own]
        copies = [
            push(part.at[lax.rem(me + step, n)], land.at[step - 1], send.at[step], recv.at[step],
                 "tensor", lax.rem(me + step, n))
            for step in range(1, n)
        ]
        total = part[me].astype(F32)
        for step, copy in enumerate(copies):
            copy.wait()
            total = total + land[step].astype(F32)
        mid = x_ref[...] + total
        mid_out[...] = mid
        xhat, _ = layer_norm(mid)
        normed_out[me] = (xhat * gain_ref[...]).astype(BF)
        copies = [
            push(normed_out.at[me], normed_out.at[me], gsend.at[step], grecv.at[step],
                 "tensor", lax.rem(me + step, n))
            for step in range(1, n)
        ]
        job.end()
        for copy in copies:
            copy.wait()

    sem = pltpu.SemaphoreType.DMA
    struct = jax.ShapeDtypeStruct
    args = (kv, starts8, q, q_start, w_out_t, x_own, gain, pack_b)
    outs = [
        struct((n, own, D), BF), struct((own, D), F32), struct((T, w), BF),
        struct((S * h, R, 1), F32), struct((n_seq,) + kv.shape, BF),
        struct((n_seq,) + starts8.shape, jnp.int32)] + job.outs
    return pl.pallas_call(
        kernel, out_shape=outs, in_specs=[VM] * len(args), out_specs=[VM] * len(outs),
        scratch_shapes=[
            pltpu.VMEM((n, own, D), BF), pltpu.VMEM((n - 1, own, D), BF),
            sem((2, n_seq)), sem((2, n_seq)), sem((2,)), sem((n,)), sem((n,)), sem((n,)), sem((n,)),
        ] + job.scratch,
        compiler_params=pltpu.CompilerParams(collective_id=cid, has_side_effects=True),
    )(*args)


def make_per_device(mesh):
    n_dp, n_seq, n_ten = mesh.shape["dp"], mesh.shape["seq"], mesh.shape["tensor"]
    sizes = (n_dp, n_seq, n_ten)
    n_all = n_dp * n_seq

    def per_device(tokens, positions, qkv_weight, attn_out_weight, mlp_in_weight, mlp_out_weight,
                   attn_gain, mlp_gain, cotangent):
        S, R = tokens.shape[:2]
        T, L = S * R, R * n_seq
        w, u = qkv_weight.shape[2], mlp_out_weight.shape[0]
        h = w // HD
        wr = qkv_weight.shape[0]
        own = T // n_ten
        pack_a = jnp.concatenate(
            [qkv_weight.reshape(wr, 3 * w), attn_out_weight.T, attn_gain[:, None], mlp_gain[:, None]],
            axis=1)
        pack_b = jnp.concatenate([mlp_in_weight.reshape(wr, 2 * u), mlp_out_weight.T], axis=1)
        full_a = gather_weights(pack_a, n_dp, n_seq, 5).reshape(D, 4 * w + 2)
        w_qkv = full_a[:, : 3 * w]
        w_out_t = full_a[:, 3 * w : 4 * w]
        gain1 = full_a[:, 4 * w].astype(F32)[None, :]
        gain2 = full_a[:, 4 * w + 1].astype(F32)[None, :]

        x = tokens.reshape(T, D)
        cot = cotangent.reshape(T, D)
        dyb = cot.astype(BF)
        t_me = lax.axis_index("tensor")
        mine = lambda a: lax.dynamic_slice_in_dim(a, t_me * own, own, 0)
        x_own, cot_own = mine(x), mine(cot)

        index = lax.axis_index("seq") * R + jnp.arange(R, dtype=jnp.int32)
        starts = index[None, :] - positions
        cosine, sine = rope_tables(positions.reshape(T))

        xhat1, _ = layer_norm(x)
        normed1 = (xhat1 * gain1).astype(BF)
        qkv = dot(normed1, w_qkv).reshape(T, 3, h, HD)
        q = rotate(qkv[:, 0], cosine, sine).astype(BF)
        k = rotate(qkv[:, 1], cosine, sine).astype(BF)
        v = qkv[:, 2].astype(BF)
        kv = jnp.concatenate([k.reshape(T, w), v.reshape(T, w)], axis=1)
        starts8 = jnp.pad(starts, ((0, 8 - S), (0, 0)))
        q_start = starts.reshape(T, 1)
        normed2, mid_own, context, lse, kv_all, starts_all, full_b = attention_stage(
            kv, starts8, q.reshape(T, w), q_start, w_out_t, x_own, gain2, pack_b, sizes, S, 1)
        full_b = full_b.reshape(D, 3 * u)
        w_in, w_down_t = full_b[:, : 2 * u], full_b[:, 2 * u :]
        normed2 = normed2.reshape(T, D)
        up = dot(normed2, w_in)
        active, slope = gelu_parts(up[:, :u])
        gate = up[:, u:]
        hidden = (active * gate).astype(BF)
        out_part = dot_t(hidden, w_down_t).astype(BF).reshape(n_ten, own, D)
        dhidden = dot(dyb, w_down_t)
        dup = jnp.concatenate([dhidden * gate * slope, dhidden * active], axis=1).astype(BF)
        dn2_part = dot_t(dup, w_in).astype(BF).reshape(n_ten, own, D)

        def after_mlp(sums, more):
            mid, dy, gain = more
            xhat2, rstd2 = layer_norm(mid)
            dn2, down = sums
            gain_grad = jnp.sum(dn2 * xhat2, axis=0, keepdims=True)
            dmid = dy + norm_backward(dn2 * gain, xhat2, rstd2)
            return [dmid, mid + down], [dmid, gain_grad]

        g_b = jnp.concatenate([t_dot(normed2, dup).astype(BF), t_dot(dyb, hidden).astype(BF)], axis=1)
        dmidb, out_rows, dmid_own, g_gain2, sum_b = sum_rows_then_gather(
            [dn2_part, out_part], [mid_own, cot_own, gain2], after_mlp,
            [((own, D), BF), ((own, D), BF)], [((own, D), F32), ((1, D), F32)],
            sizes, [GradScatter(g_b.reshape(n_all, wr, 3 * u), n_dp, n_seq)], 2)
        output = out_rows.astype(F32).reshape(S, R, D)
        dmidb = dmidb.reshape(T, D)
        dcontext = dot(dmidb, w_out_t).astype(BF)
        k_start = jnp.transpose(starts_all[:, :S], (1, 0, 2)).reshape(S, L)
        kv_heads = jnp.transpose(
            kv_all.reshape(n_seq, S, R, 2, h, HD), (3, 1, 4, 0, 2, 5)).reshape(2, S, h, L, HD)
        keys, values = kv_heads[0], kv_heads[1]
        qh = jnp.transpose(q.reshape(S, R, h, HD), (0, 2, 1, 3))
        ctx_h = jnp.transpose(context.reshape(S, R, h, HD), (0, 2, 1, 3))
        scale = 1.0 / math.sqrt(HD)
        mask = (starts[:, :, None] == k_start[:, None, :])[:, None]
        scores = jnp.einsum("shqd,shkd->shqk", qh, keys, preferred_element_type=F32) * scale
        scores = jnp.where(mask, scores, -jnp.inf)
        probs32 = jnp.exp(scores - lse.reshape(S, h, R, 1))
        probs = probs32.astype(BF)
        dch = jnp.transpose(dcontext.reshape(S, R, h, HD), (0, 2, 1, 3))
        delta = jnp.sum(dch.astype(F32) * ctx_h.astype(F32), axis=-1, keepdims=True)
        dprobs = jnp.einsum("shqd,shkd->shqk", dch, values, preferred_element_type=F32)
        dscores = (probs32 * (dprobs - delta) * scale).astype(BF)
        dqh = jnp.einsum("shqk,shkd->shqd", dscores, keys, preferred_element_type=F32)
        dkh = jnp.einsum("shqk,shqd->shkd", dscores, qh, preferred_element_type=F32)
        dvh = jnp.einsum("shqk,shqd->shkd", probs, dch, preferred_element_type=F32)
        dkv = jnp.stack([dkh, dvh]).astype(BF).reshape(2, S, h, n_seq, R, HD)
        dkv = jnp.transpose(dkv, (3, 1, 4, 0, 2, 5)).reshape(n_seq, T, 2 * w)
        dkv_own = scatter_sum(dkv, "seq", n_seq, 3)
        dq = unrotate(jnp.transpose(dqh, (0, 2, 1, 3)).reshape(T, h, HD), cosine, sine)
        dk = unrotate(dkv_own[:, :w].reshape(T, h, HD), cosine, sine)
        dqkv = jnp.concatenate(
            [dq.reshape(T, w), dk.reshape(T, w), dkv_own[:, w:]], axis=1).astype(BF)
        dn1_part = dot_t(dqkv, w_qkv)
        g_gain1 = jnp.sum(dn1_part * xhat1, axis=0)
        dn1_part = dn1_part.astype(BF).reshape(n_ten, own, D)
        gain_grads = jnp.stack([g_gain1, g_gain2[0]]).reshape(2, n_all, wr)
        gain_grads = jnp.pad(jnp.transpose(gain_grads, (1, 0, 2)), ((0, 0), (0, 6), (0, 128 - wr)))
        g_a = jnp.concatenate([t_dot(normed1, dqkv).astype(BF), t_dot(dmidb, context).astype(BF)], axis=1)

        def at_the_end(sums, more):
            rows, dmid, gain = more
            xhat, rstd = layer_norm(rows)
            return [dmid + norm_backward(sums[0] * gain, xhat, rstd)], []

        grad_rows, sum_a, gains = sum_rows_then_gather(
            [dn1_part], [x_own, dmid_own, gain1], at_the_end,
            [((own, D), BF)], [], sizes,
            [GradScatter(g_a.reshape(n_all, wr, 4 * w), n_dp, n_seq),
             GainSum(gain_grads, n_dp, n_seq, n_ten)], 4)
        grad_tokens = grad_rows.astype(F32).reshape(S, R, D)
        return (
            output,
            grad_tokens,
            sum_a[:, : 3 * w].reshape(wr, 3, w),
            sum_a[:, 3 * w :].T,
            sum_b[:, : 2 * u].reshape(wr, 2, u),
            sum_b[:, 2 * u :].T,
            gains[0, :wr],
            gains[1, :wr],
        )

    return per_device


def solution(mesh):
    rows = P("dp", "seq", None)
    group = ("dp", "seq")
    weights = (P(group, None, "tensor"), P("tensor", group), P(group, None, "tensor"),
               P("tensor", group), P(group), P(group))
    return jax.shard_map(
        make_per_device(mesh), mesh=mesh,
        in_specs=(rows, P("dp", "seq")) + weights + (rows,),
        out_specs=(rows, rows) + weights,
        check_vma=False,
    )
```

```python
import math

import jax
import jax.numpy as jnp
from jax import lax
from jax.experimental import pallas as pl
from jax.experimental.pallas import tpu as pltpu
from jax.sharding import PartitionSpec as P

D = 768
HD = 64
EPS = 1e-05
ROPE_BASE = 160000.0
INV_ROOT2 = 0.7071067811865476
INV_ROOT2PI = 0.3989422804014327
MESH = pl.DeviceIdType.MESH
BF = jnp.bfloat16
F32 = jnp.float32
VM = pl.BlockSpec(memory_space=pltpu.VMEM)


def layer_norm(values):
    mean = jnp.mean(values, axis=-1, keepdims=True)
    centred = values - mean
    inverse = lax.rsqrt(jnp.mean(centred * centred, axis=-1, keepdims=True) + EPS)
    return centred * inverse, inverse


def norm_backward(e, xhat, r):
    first = jnp.mean(e, axis=-1, keepdims=True)
    second = jnp.mean(e * xhat, axis=-1, keepdims=True)
    return r * (e - first - xhat * second)


def rope_tables(places):
    half = HD // 2
    ramp = jnp.arange(half, dtype=F32) * (2.0 / HD)
    freq = jnp.exp(-math.log(ROPE_BASE) * ramp)
    angle = places.astype(F32)[:, None] * freq[None, :]
    cosine, sine = jnp.cos(angle), jnp.sin(angle)
    return jnp.concatenate([cosine, cosine], axis=-1), jnp.concatenate([sine, sine], axis=-1)


def rotate(values, cosine, sine):
    half = HD // 2
    turned = jnp.concatenate([-values[..., half:], values[..., :half]], axis=-1)
    return values * cosine[:, None, :] + turned * sine[:, None, :]


def unrotate(grads, cosine, sine):
    half = HD // 2
    moved = grads * sine[:, None, :]
    back = jnp.concatenate([moved[..., half:], -moved[..., :half]], axis=-1)
    return grads * cosine[:, None, :] + back


def gelu_parts(a):
    cdf = 0.5 * (1.0 + lax.erf(a * INV_ROOT2))
    return a * cdf, cdf + a * jnp.exp(-0.5 * a * a) * INV_ROOT2PI


def greet(*names_and_sizes):
    barrier = pltpu.get_barrier_semaphore()
    count = 0
    for axis, n in names_and_sizes:
        me = lax.axis_index(axis)
        for step in range(1, n):
            pl.semaphore_signal(
                barrier, inc=1, device_id={axis: lax.rem(me + step, n)}, device_id_type=MESH
            )
            count += 1
    pl.semaphore_wait(barrier, count)


def push(src, dst, send, recv, axis, peer):
    copy = pltpu.make_async_remote_copy(
        src_ref=src, dst_ref=dst, send_sem=send, recv_sem=recv,
        device_id={axis: peer}, device_id_type=MESH,
    )
    copy.start()
    return copy


class WeightGather:
    def __init__(self, array, n_dp, n_seq):
        self.array, self.n_dp, self.n_seq = array, n_dp, n_seq
        self.outs = [jax.ShapeDtypeStruct((n_dp * n_seq,) + array.shape, array.dtype)]
        sem = pltpu.SemaphoreType.DMA
        self.scratch = [sem((n_seq,)), sem((n_seq,)), sem((n_dp, n_seq)), sem((n_dp, n_seq)), sem((1,))]

    def across(self, src, block, step):
        dp = lax.axis_index("dp")
        return [
            push(src, self.out.at[block], self.xs.at[k, step], self.xr.at[k, step], "dp",
                 lax.rem(dp + k, self.n_dp))
            for k in range(1, self.n_dp)
        ]

    def begin(self, src, outs, scratch):
        (self.out,) = outs
        zs, zr, self.xs, self.xr, local = scratch
        seq = lax.axis_index("seq")
        self.base = lax.axis_index("dp") * self.n_seq
        block = self.base + seq
        self.along = [
            push(src, self.out.at[block], zs.at[step], zr.at[step], "seq",
                 lax.rem(seq + step, self.n_seq))
            for step in range(1, self.n_seq)
        ]
        self.crossing = self.across(src, block, 0)
        self.own = pltpu.make_async_copy(src, self.out.at[block], local.at[0])
        self.own.start()

    def end(self):
        seq = lax.axis_index("seq")
        for step, copy in enumerate(self.along, 1):
            copy.wait_recv()
            block = self.base + lax.rem(seq + self.n_seq - step, self.n_seq)
            self.crossing += self.across(self.out.at[block], block, step)
        for copy in self.along:
            copy.wait_send()
        for copy in self.crossing:
            copy.wait()
        self.own.wait()


class GradScatter:
    def __init__(self, array, n_dp, n_seq):
        self.array, self.n_dp, self.n_seq = array, n_dp, n_seq
        shape, kind = array.shape[1:], array.dtype
        self.outs = [jax.ShapeDtypeStruct(shape, F32)]
        sem = pltpu.SemaphoreType.DMA
        self.scratch = [
            pltpu.VMEM((n_dp - 1, n_seq) + shape, kind),
            pltpu.VMEM((n_seq,) + shape, kind),
            pltpu.VMEM((n_seq,) + shape, kind),
            sem((n_dp, n_seq)), sem((n_dp, n_seq)), sem((n_seq,)), sem((n_seq,)),
        ]

    def begin(self, src, outs, scratch):
        self.src, (self.out,) = src, outs
        self.landx, self.stage, self.landz, xs, xr, self.zs, self.zr = scratch
        dp, seq = lax.axis_index("dp"), lax.axis_index("seq")
        self.crossing = {}
        for step in list(range(1, self.n_seq)) + [0]:
            to = lax.rem(seq + step, self.n_seq)
            self.crossing[step] = [
                push(src.at[lax.rem(dp + k, self.n_dp) * self.n_seq + to],
                     self.landx.at[k - 1, step], xs.at[k, step], xr.at[k, step], "dp",
                     lax.rem(dp + k, self.n_dp))
                for k in range(1, self.n_dp)
            ]

    def end(self):
        dp, seq = lax.axis_index("dp"), lax.axis_index("seq")
        along = []
        for step in list(range(1, self.n_seq)) + [0]:
            to = lax.rem(seq + step, self.n_seq)
            total = self.src[dp * self.n_seq + to].astype(F32)
            for k, copy in enumerate(self.crossing[step]):
                copy.wait()
                total = total + self.landx[k, step].astype(F32)
            if step:
                self.stage[step] = total.astype(self.stage.dtype)
                along.append(
                    push(self.stage.at[step], self.landz.at[step], self.zs.at[step],
                         self.zr.at[step], "seq", to))
        for step, copy in enumerate(along, 1):
            copy.wait()
            total = total + self.landz[step].astype(F32)
        self.out[...] = total


class GainSum:
    def __init__(self, array, n_dp, n_seq, n_ten):
        self.array, self.sizes = array, (n_ten, n_dp, n_seq)
        shape = array.shape[1:]
        self.outs = [jax.ShapeDtypeStruct(shape, F32)]
        sem = pltpu.SemaphoreType.DMA
        self.scratch = [
            pltpu.VMEM((n_ten,) + array.shape, F32),
            pltpu.VMEM(array.shape, F32),
            pltpu.VMEM((n_dp, n_seq) + shape, F32),
            pltpu.VMEM((n_seq,) + shape, F32),
            pltpu.VMEM((n_seq,) + shape, F32),
        ] + [sem((n,)) for n in (n_ten, n_ten, n_seq, n_seq)] + [sem((n_dp, n_seq))] * 2

    def begin(self, src, outs, scratch):
        self.src, (self.out,) = src, outs
        (self.land, self.total, self.landx, self.stage, self.landz,
         ys, yr, self.zs, self.zr, self.xs, self.xr) = scratch
        n_ten = self.sizes[0]
        me = lax.axis_index("tensor")
        self.first = [
            push(src, self.land.at[step], ys.at[step], yr.at[step], "tensor",
                 lax.rem(me + step, n_ten))
            for step in range(1, n_ten)
        ]

    def between(self):
        _, n_dp, n_seq = self.sizes
        dp, seq = lax.axis_index("dp"), lax.axis_index("seq")
        total = self.src[...]
        for step, copy in enumerate(self.first, 1):
            copy.wait()
            total = total + self.land[step]
        self.total[...] = total
        self.crossing = {
            step: [
                push(self.total.at[lax.rem(dp + k, n_dp) * n_seq + lax.rem(seq + step, n_seq)],
                     self.landx.at[k, step], self.xs.at[k, step], self.xr.at[k, step], "dp",
                     lax.rem(dp + k, n_dp))
                for k in range(1, n_dp)
            ]
            for step in range(n_seq)
        }

    def end(self):
        _, n_dp, n_seq = self.sizes
        dp, seq = lax.axis_index("dp"), lax.axis_index("seq")
        along = []
        for step in list(range(1, n_seq)) + [0]:
            to = lax.rem(seq + step, n_seq)
            total = self.total[dp * n_seq + to]
            for k, copy in enumerate(self.crossing[step], 1):
                copy.wait()
                total = total + self.landx[k, step]
            if step:
                self.stage[step] = total
                along.append(
                    push(self.stage.at[step], self.landz.at[step], self.zs.at[step],
                         self.zr.at[step], "seq", to))
        for step, copy in enumerate(along, 1):
            copy.wait()
            total = total + self.landz[step]
        self.out[...] = total


def gather_weights(array, n_dp, n_seq, cid):
    job = WeightGather(array, n_dp, n_seq)

    def kernel(src, out, *scratch):
        greet(("dp", n_dp), ("seq", n_seq))
        job.begin(src, [out], scratch)
        job.end()

    return pl.pallas_call(
        kernel, out_shape=job.outs[0], in_specs=[VM], out_specs=VM, scratch_shapes=job.scratch,
        compiler_params=pltpu.CompilerParams(collective_id=cid, has_side_effects=True),
    )(array)


def sum_rows_then_gather(partials, extras, middle, gathered, owned, sizes, jobs, cid):
    n_dp, n_seq, n = sizes
    np_, ne, ng, no, nj = len(partials), len(extras), len(gathered), len(owned), len(jobs)
    rows = partials[0].shape[1:]

    def kernel(*refs):
        refs = list(refs)
        take = lambda k: [refs.pop(0) for _ in range(k)]
        parts, more, srcs = take(np_), take(ne), take(nj)
        gouts, oouts, jouts = take(ng), take(no), take(nj)
        lands, (send, recv, gsend, grecv) = take(np_), take(4)
        greet(("dp", n_dp), ("seq", n_seq), ("tensor", n))
        me = lax.axis_index("tensor")
        copies = []
        for i in range(np_):
            copies.append([
                push(parts[i].at[lax.rem(me + step, n)], lands[i].at[step - 1], send.at[i, step],
                     recv.at[i, step], "tensor", lax.rem(me + step, n))
                for step in range(1, n)
            ])
        for job, src, out in zip(jobs, srcs, jouts):
            job.begin(src, [out], take(len(job.scratch)))
        sums = []
        for i in range(np_):
            total = parts[i][me].astype(F32)
            for step, copy in enumerate(copies[i]):
                copy.wait()
                total = total + lands[i][step].astype(F32)
            sums.append(total)
        shared, kept = middle(sums, [m[...] for m in more])
        copies = []
        for i in range(ng):
            gouts[i][me] = shared[i].astype(gathered[i][1])
            for step in range(1, n):
                copies.append(
                    push(gouts[i].at[me], gouts[i].at[me], gsend.at[i, step], grecv.at[i, step],
                         "tensor", lax.rem(me + step, n))
                )
        for i in range(no):
            oouts[i][...] = kept[i].astype(owned[i][1])
        for job in jobs:
            if isinstance(job, GainSum):
                job.between()
        for job in jobs:
            job.end()
        for copy in copies:
            copy.wait()

    sem = pltpu.SemaphoreType.DMA
    return pl.pallas_call(
        kernel,
        out_shape=[jax.ShapeDtypeStruct((n,) + s, t) for s, t in gathered]
        + [jax.ShapeDtypeStruct(s, t) for s, t in owned]
        + [job.outs[0] for job in jobs],
        in_specs=[VM] * (np_ + ne + nj),
        out_specs=[VM] * (ng + no + nj),
        scratch_shapes=[pltpu.VMEM((n - 1,) + rows, p.dtype) for p in partials]
        + [sem((np_, n)), sem((np_, n)), sem((ng, n)), sem((ng, n))]
        + [scratch for job in jobs for scratch in job.scratch],
        compiler_params=pltpu.CompilerParams(collective_id=cid, has_side_effects=True),
    )(*partials, *extras, *[job.array for job in jobs])


def dot(a, b):
    return jnp.dot(a, b, preferred_element_type=F32)


def dot_t(a, b):
    return lax.dot_general(a, b, (((1,), (1,)), ((), ())), preferred_element_type=F32)


def t_dot(a, b):
    return lax.dot_general(a, b, (((0,), (0,)), ((), ())), preferred_element_type=F32)


def attention_stage(kv, starts8, q, q_start, w_out_t, x_own, gain, pack_b, sizes, S, cid):
    n_dp, n_seq, n = sizes
    T, w = q.shape
    R, h, own = T // S, w // HD, x_own.shape[0]
    L = R * n_seq
    scale = 1.0 / math.sqrt(HD)
    job = WeightGather(pack_b, n_dp, n_seq)

    def kernel(kv_ref, st_ref, q_ref, qs_ref, wo_ref, x_ref, gain_ref, pb_ref,
               normed_out, mid_out, ctx_out, lse_out, kv_all, st_all, pb_out,
               part, land, ksend, krecv, local, send, recv, gsend, grecv, *rest):
        greet(("dp", n_dp), ("seq", n_seq), ("tensor", n))
        me, seq = lax.axis_index("tensor"), lax.axis_index("seq")
        arriving = []
        for i, (src, dst) in enumerate(((st_ref, st_all), (kv_ref, kv_all))):
            for step in range(1, n_seq):
                arriving.append(
                    push(src, dst.at[seq], ksend.at[i, step], krecv.at[i, step], "seq",
                         lax.rem(seq + step, n_seq)))
            mine = pltpu.make_async_copy(src, dst.at[seq], local.at[i])
            mine.start()
            mine.wait()
        job.begin(pb_ref, [pb_out], rest)
        for copy in arriving:
            copy.wait()
        for s in range(S):
            rows = slice(s * R, (s + 1) * R)
            k_start = jnp.concatenate([st_all[j, s : s + 1, :] for j in range(n_seq)], axis=1)
            same = qs_ref[rows, :] == k_start
            heads = []
            for i in range(h):
                cols = slice(i * HD, (i + 1) * HD)
                keys = kv_all[:, rows, cols].reshape(L, HD)
                values = kv_all[:, rows, w + i * HD : w + (i + 1) * HD].reshape(L, HD)
                scores = jnp.where(same, dot_t(q_ref[rows, cols], keys) * scale, -jnp.inf)
                top = jnp.max(scores, axis=-1, keepdims=True)
                lse = top + jnp.log(jnp.sum(jnp.exp(scores - top), axis=-1, keepdims=True))
                lse_out[s * h + i] = lse
                probs = jnp.exp(scores - lse).astype(BF)
                heads.append(dot(probs, values).astype(BF))
            ctx_out[rows, :] = jnp.concatenate(heads, axis=1)
        projected = dot_t(ctx_out[...], wo_ref[...]).astype(BF)
        for i in range(n):
            part[i] = projected[i * own : (i + 1) * own]
        copies = [
            push(part.at[lax.rem(me + step, n)], land.at[step - 1], send.at[step], recv.at[step],
                 "tensor", lax.rem(me + step, n))
            for step in range(1, n)
        ]
        total = part[me].astype(F32)
        for step, copy in enumerate(copies):
            copy.wait()
            total = total + land[step].astype(F32)
        mid = x_ref[...] + total
        mid_out[...] = mid
        xhat, _ = layer_norm(mid)
        normed_out[me] = (xhat * gain_ref[...]).astype(BF)
        copies = [
            push(normed_out.at[me], normed_out.at[me], gsend.at[step], grecv.at[step],
                 "tensor", lax.rem(me + step, n))
            for step in range(1, n)
        ]
        job.end()
        for copy in copies:
            copy.wait()

    sem = pltpu.SemaphoreType.DMA
    struct = jax.ShapeDtypeStruct
    args = (kv, starts8, q, q_start, w_out_t, x_own, gain, pack_b)
    outs = [
        struct((n, own, D), BF), struct((own, D), F32), struct((T, w), BF),
        struct((S * h, R, 1), F32), struct((n_seq,) + kv.shape, BF),
        struct((n_seq,) + starts8.shape, jnp.int32)] + job.outs
    return pl.pallas_call(
        kernel, out_shape=outs, in_specs=[VM] * len(args), out_specs=[VM] * len(outs),
        scratch_shapes=[
            pltpu.VMEM((n, own, D), BF), pltpu.VMEM((n - 1, own, D), BF),
            sem((2, n_seq)), sem((2, n_seq)), sem((2,)), sem((n,)), sem((n,)), sem((n,)), sem((n,)),
        ] + job.scratch,
        compiler_params=pltpu.CompilerParams(collective_id=cid, has_side_effects=True),
    )(*args)


def attention_backward(q, dcontext, context, kv_all, st_all, q_start, lse, sizes, S, cid):
    _, n_seq, _ = sizes
    T, w = q.shape
    R, h = T // S, w // HD
    L = R * n_seq
    scale = 1.0 / math.sqrt(HD)

    def kernel(q_ref, dc_ref, ctx_ref, kv_ref, st_ref, qs_ref, lse_ref, dq_out, dkv_out,
               block, land, send, recv):
        greet(("seq", n_seq))
        seq = lax.axis_index("seq")
        for s in range(S):
            rows = slice(s * R, (s + 1) * R)
            k_start = jnp.concatenate([st_ref[j, s : s + 1, :] for j in range(n_seq)], axis=1)
            same = qs_ref[rows, :] == k_start
            dqs, dks, dvs = [], [], []
            for i in range(h):
                cols = slice(i * HD, (i + 1) * HD)
                keys = kv_ref[:, rows, cols].reshape(L, HD)
                values = kv_ref[:, rows, w + i * HD : w + (i + 1) * HD].reshape(L, HD)
                query, dc = q_ref[rows, cols], dc_ref[rows, cols]
                delta = jnp.sum(
                    dc.astype(F32) * ctx_ref[rows, cols].astype(F32), axis=-1, keepdims=True)
                scores = jnp.where(same, dot_t(query, keys) * scale, -jnp.inf)
                probs = jnp.exp(scores - lse_ref[s * h + i])
                dscores = (probs * (dot_t(dc, values) - delta) * scale).astype(BF)
                dqs.append(dot(dscores, keys))
                dks.append(t_dot(dscores, query).astype(BF))
                dvs.append(t_dot(probs.astype(BF), dc).astype(BF))
            dq_out[rows, :] = jnp.concatenate(dqs, axis=1)
            block[:, rows, :] = jnp.concatenate(dks + dvs, axis=1).reshape(n_seq, R, 2 * w)
        copies = [
            push(block.at[lax.rem(seq + step, n_seq)], land.at[step - 1], send.at[step],
                 recv.at[step], "seq", lax.rem(seq + step, n_seq))
            for step in range(1, n_seq)
        ]
        total = block[seq].astype(F32)
        for step, copy in enumerate(copies):
            copy.wait()
            total = total + land[step].astype(F32)
        dkv_out[...] = total

    sem = pltpu.SemaphoreType.DMA
    args = (q, dcontext, context, kv_all, st_all, q_start, lse)
    return pl.pallas_call(
        kernel,
        out_shape=[jax.ShapeDtypeStruct((T, w), F32), jax.ShapeDtypeStruct((T, 2 * w), F32)],
        in_specs=[VM] * len(args), out_specs=[VM] * 2,
        scratch_shapes=[
            pltpu.VMEM((n_seq, T, 2 * w), BF), pltpu.VMEM((n_seq - 1, T, 2 * w), BF),
            sem((n_seq,)), sem((n_seq,)),
        ],
        compiler_params=pltpu.CompilerParams(collective_id=cid, has_side_effects=True),
    )(*args)


def make_per_device(mesh):
    n_dp, n_seq, n_ten = mesh.shape["dp"], mesh.shape["seq"], mesh.shape["tensor"]
    sizes = (n_dp, n_seq, n_ten)
    n_all = n_dp * n_seq

    def per_device(tokens, positions, qkv_weight, attn_out_weight, mlp_in_weight, mlp_out_weight,
                   attn_gain, mlp_gain, cotangent):
        S, R = tokens.shape[:2]
        T, L = S * R, R * n_seq
        w, u = qkv_weight.shape[2], mlp_out_weight.shape[0]
        h = w // HD
        wr = qkv_weight.shape[0]
        own = T // n_ten
        pack_a = jnp.concatenate(
            [qkv_weight.reshape(wr, 3 * w), attn_out_weight.T, attn_gain[:, None], mlp_gain[:, None]],
            axis=1)
        pack_b = jnp.concatenate([mlp_in_weight.reshape(wr, 2 * u), mlp_out_weight.T], axis=1)
        full_a = gather_weights(pack_a, n_dp, n_seq, 5).reshape(D, 4 * w + 2)
        w_qkv = full_a[:, : 3 * w]
        w_out_t = full_a[:, 3 * w : 4 * w]
        gain1 = full_a[:, 4 * w].astype(F32)[None, :]
        gain2 = full_a[:, 4 * w + 1].astype(F32)[None, :]

        x = tokens.reshape(T, D)
        cot = cotangent.reshape(T, D)
        dyb = cot.astype(BF)
        t_me = lax.axis_index("tensor")
        mine = lambda a: lax.dynamic_slice_in_dim(a, t_me * own, own, 0)
        x_own, cot_own = mine(x), mine(cot)

        index = lax.axis_index("seq") * R + jnp.arange(R, dtype=jnp.int32)
        starts = index[None, :] - positions
        cosine, sine = rope_tables(positions.reshape(T))

        xhat1, _ = layer_norm(x)
        normed1 = (xhat1 * gain1).astype(BF)
        qkv = dot(normed1, w_qkv).reshape(T, 3, h, HD)
        q = rotate(qkv[:, 0], cosine, sine).astype(BF)
        k = rotate(qkv[:, 1], cosine, sine).astype(BF)
        v = qkv[:, 2].astype(BF)
        kv = jnp.concatenate([k.reshape(T, w), v.reshape(T, w)], axis=1)
        starts8 = jnp.pad(starts, ((0, 8 - S), (0, 0)))
        q_start = starts.reshape(T, 1)
        normed2, mid_own, context, lse, kv_all, starts_all, full_b = attention_stage(
            kv, starts8, q.reshape(T, w), q_start, w_out_t, x_own, gain2, pack_b, sizes, S, 1)
        full_b = full_b.reshape(D, 3 * u)
        w_in, w_down_t = full_b[:, : 2 * u], full_b[:, 2 * u :]
        normed2 = normed2.reshape(T, D)
        up = dot(normed2, w_in)
        active, slope = gelu_parts(up[:, :u])
        gate = up[:, u:]
        hidden = (active * gate).astype(BF)
        out_part = dot_t(hidden, w_down_t).astype(BF).reshape(n_ten, own, D)
        dhidden = dot(dyb, w_down_t)
        dup = jnp.concatenate([dhidden * gate * slope, dhidden * active], axis=1).astype(BF)
        dn2_part = dot_t(dup, w_in).astype(BF).reshape(n_ten, own, D)

        def after_mlp(sums, more):
            mid, dy, gain = more
            xhat2, rstd2 = layer_norm(mid)
            dn2, down = sums
            gain_grad = jnp.sum(dn2 * xhat2, axis=0, keepdims=True)
            dmid = dy + norm_backward(dn2 * gain, xhat2, rstd2)
            return [dmid, mid + down], [dmid, gain_grad]

        g_b = jnp.concatenate([t_dot(normed2, dup).astype(BF), t_dot(dyb, hidden).astype(BF)], axis=1)
        dmidb, out_rows, dmid_own, g_gain2, sum_b = sum_rows_then_gather(
            [dn2_part, out_part], [mid_own, cot_own, gain2], after_mlp,
            [((own, D), BF), ((own, D), BF)], [((own, D), F32), ((1, D), F32)],
            sizes, [GradScatter(g_b.reshape(n_all, wr, 3 * u), n_dp, n_seq)], 2)
        output = out_rows.astype(F32).reshape(S, R, D)
        dmidb = dmidb.reshape(T, D)
        dcontext = dot(dmidb, w_out_t).astype(BF)
        dq_rows, dkv_own = attention_backward(
            q.reshape(T, w), dcontext, context, kv_all, starts_all, q_start, lse, sizes, S, 3)
        dq = unrotate(dq_rows.reshape(T, h, HD), cosine, sine)
        dk = unrotate(dkv_own[:, :w].reshape(T, h, HD), cosine, sine)
        dqkv = jnp.concatenate(
            [dq.reshape(T, w), dk.reshape(T, w), dkv_own[:, w:]], axis=1).astype(BF)
        dn1_part = dot_t(dqkv, w_qkv)
        g_gain1 = jnp.sum(dn1_part * xhat1, axis=0)
        dn1_part = dn1_part.astype(BF).reshape(n_ten, own, D)
        gain_grads = jnp.stack([g_gain1, g_gain2[0]]).reshape(2, n_all, wr)
        gain_grads = jnp.pad(jnp.transpose(gain_grads, (1, 0, 2)), ((0, 0), (0, 6), (0, 128 - wr)))
        g_a = jnp.concatenate([t_dot(normed1, dqkv).astype(BF), t_dot(dmidb, context).astype(BF)], axis=1)

        def at_the_end(sums, more):
            rows, dmid, gain = more
            xhat, rstd = layer_norm(rows)
            return [dmid + norm_backward(sums[0] * gain, xhat, rstd)], []

        grad_rows, sum_a, gains = sum_rows_then_gather(
            [dn1_part], [x_own, dmid_own, gain1], at_the_end,
            [((own, D), BF)], [], sizes,
            [GradScatter(g_a.reshape(n_all, wr, 4 * w), n_dp, n_seq),
             GainSum(gain_grads, n_dp, n_seq, n_ten)], 4)
        grad_tokens = grad_rows.astype(F32).reshape(S, R, D)
        return (
            output,
            grad_tokens,
            sum_a[:, : 3 * w].reshape(wr, 3, w),
            sum_a[:, 3 * w :].T,
            sum_b[:, : 2 * u].reshape(wr, 2, u),
            sum_b[:, 2 * u :].T,
            gains[0, :wr],
            gains[1, :wr],
        )

    return per_device


def solution(mesh):
    rows = P("dp", "seq", None)
    group = ("dp", "seq")
    weights = (P(group, None, "tensor"), P("tensor", group), P(group, None, "tensor"),
               P("tensor", group), P(group), P(group))
    return jax.shard_map(
        make_per_device(mesh), mesh=mesh,
        in_specs=(rows, P("dp", "seq")) + weights + (rows,),
        out_specs=(rows, rows) + weights,
        check_vma=False,
    )
```
